32 devices in a mesh: clip: 4 (over z), frame: 4 (over x, core), row: 2 (over y).
Axes of the slice: x: 2, y: 2, z: 4, core: 2. Of those that a mesh axis runs over, the one named last changes fastest.
Arguments:
- features: bfloat16 [4, 16, 2, 32, 384], P('clip', 'frame', 'row'), may hold values from -6 to 6
- time_weight: bfloat16 [3, 384, 768], replicated, may hold values from -0.1875 to 0.1875
- time_bias: float32 [768], replicated, may hold values from -3 to 3
- space_weight: bfloat16 [3, 3, 384, 192], replicated, may hold values from -0.109375 to 0.109375
- pixel_grads: bfloat16 [4, 32, 4, 64, 192], P('clip', ('frame', 'row')), may hold values from -6 to 6
- frame_order: int32 [4, 4, 8], P('clip', 'frame'), may hold values from 0 to 7, each once within a row
Outputs:
- input_grad: bfloat16 [4, 16, 2, 32, 384], P('clip', 'frame', 'row')
- weight_grad: float32 [663552], P(('frame', 'row'))
The draws below stay inside these ranges and needn't reach their ends.
Inputs may be any that keep to these rules, and one draw needn't show every extreme that they name: `frame_order`: for each clip and frame group, the row lists every one of the group's 8 output frames exactly once.
All inputs are finite; a program needn't handle non-finite values.
Results may differ from the reference program's by a relative error of at most 0.0049.
Values may be sent and summed in bfloat16 or wider, within the bound.
No kernel may reach another device: no remote copies, remote signals or barrier semaphores. Data moves between devices by JAX's collectives and lax.ppermute only.
A program may use at most 64 MiB of HBM per device.

```python
import math
import jax
import jax.numpy as jnp
from jax import lax

C = 384
CO = 192
W = 32
CLIPS = 4
FRAMES = 16
HEIGHT = 2
OF_DEV = 8
OUT_PIX = 32768
N_FRAME = 4


def levels(own_key, shape, cuts, low, largest):
    def one(dim, parts):
        heights = jax.random.uniform(jax.random.fold_in(jax.random.fold_in(own_key, 6), dim), (parts,), jnp.float32, low / len(cuts), largest / len(cuts))
        return jnp.repeat(jnp.exp(heights), shape[dim] // parts).reshape((-1,) + (1,) * (len(shape) - dim - 1))

    level = one(*cuts[0])
    for cut in cuts[1:]:
        level = level * one(*cut)
    return level


def scatter_about(stream_key, shape, width, limit, cuts=(), dtype=jnp.bfloat16):
    result = width * jax.random.normal(stream_key, shape, jnp.float32)
    if cuts:
        result = result * levels(stream_key, shape, cuts, -0.22, 0.18)
    return jnp.clip(result, -limit, limit).astype(dtype)


def setup_inputs(seed: int = 0) -> dict:
    key_of = jax.random.split(jax.random.key(seed), 7)
    return {
        "features": scatter_about(key_of[0], (CLIPS, FRAMES, HEIGHT, W, C), 1.0, 6.0, ((0, 4), (1, 4), (2, 2))),
        "time_weight": scatter_about(key_of[1], (3, C, 2 * C), (3 * C) ** -0.5, 0.1875),
        "time_bias": scatter_about(key_of[2], (2 * C,), 0.5, 3.0, (), jnp.float32),
        "space_weight": scatter_about(key_of[3], (3, 3, C, CO), (9 * C) ** -0.5, 0.109375),
        "pixel_grads": scatter_about(key_of[4], (CLIPS, 2 * FRAMES, 2 * HEIGHT, 2 * W, CO), 1.0, 6.0, ((0, 4), (1, 8))),
        "frame_order": jax.vmap(lambda own: jax.random.permutation(own, OF_DEV))(jax.random.split(key_of[5], CLIPS * N_FRAME)).reshape((CLIPS, N_FRAME, OF_DEV)).astype(jnp.int32),
    }


def one_clip(items, time_weight, time_bias, space_weight):
    feat, stored, order = items
    place = (jnp.arange(N_FRAME)[:, None] * OF_DEV + order).reshape(-1).astype(jnp.int32)
    grads = jnp.zeros_like(stored).at[place].set(stored)
    flat = FRAMES * HEIGHT * W
    up_height = 2 * HEIGHT
    up_width = 2 * W
    npix = 2 * FRAMES * up_height * up_width
    padded_feat = jnp.pad(feat, ((2, 0), (0, 0), (0, 0), (0, 0)))
    act = jnp.zeros((flat, 2 * C), jnp.float32) + time_bias.astype(jnp.float32)
    for offset in range(3):
        act = act + jnp.dot(padded_feat[offset:offset + FRAMES].reshape(flat, C), time_weight[offset], preferred_element_type=jnp.float32)
    act = act.astype(jnp.bfloat16).reshape(FRAMES, HEIGHT, W, 2 * C)
    upsampled = jnp.stack((act[..., :C], act[..., C:]), axis=1).reshape(2 * FRAMES, HEIGHT, W, C)
    upsampled = jnp.repeat(jnp.repeat(upsampled, 2, axis=1), 2, axis=2)
    padded_up = jnp.pad(upsampled, ((0, 0), (1, 1), (1, 1), (0, 0)))
    grad_flat = grads.reshape(npix, CO)
    tap_terms = []
    for tap_row in range(3):
        for tap_col in range(3):
            window = padded_up[:, tap_row:tap_row + up_height, tap_col:tap_col + up_width].reshape(npix, C)
            tap_terms.append(jnp.dot(window.T, grad_flat, preferred_element_type=jnp.float32))
    padded_grad = jnp.pad(grads, ((0, 0), (1, 1), (1, 1), (0, 0)))
    up_grad = jnp.zeros((npix, C), jnp.float32)
    for tap_row in range(3):
        for tap_col in range(3):
            window = padded_grad[:, 2 - tap_row:2 - tap_row + up_height, 2 - tap_col:2 - tap_col + up_width].reshape(npix, CO)
            up_grad = up_grad + jnp.dot(window, space_weight[tap_row, tap_col].T, preferred_element_type=jnp.float32)
    pooled = up_grad.reshape(FRAMES, 2, HEIGHT, 2, W, 2, C).sum(axis=(3, 5))
    act_grad = pooled.transpose(0, 2, 3, 1, 4).reshape(FRAMES, HEIGHT, W, 2 * C).astype(jnp.bfloat16)
    tail = jnp.pad(act_grad, ((0, 2), (0, 0), (0, 0), (0, 0)))
    input_grad = jnp.zeros((flat, C), jnp.float32)
    for offset in range(3):
        input_grad = input_grad + jnp.dot(tail[2 - offset:2 - offset + FRAMES].reshape(flat, 2 * C), time_weight[offset].T, preferred_element_type=jnp.float32)
    input_grad = input_grad.astype(jnp.bfloat16).reshape(FRAMES, HEIGHT, W, C)
    return (input_grad, jnp.stack(tap_terms).reshape(-1))

def reference(features, time_weight, time_bias, space_weight, pixel_grads, frame_order):

    def per_clip(items):
        return one_clip(items, time_weight, time_bias, space_weight)
    input_grad, terms = lax.map(per_clip, (features, pixel_grads, frame_order))
    weight_grad = lax.optimization_barrier(jnp.sum(terms, axis=0)) * (1.0 / math.sqrt(OUT_PIX))
    return (input_grad, weight_grad)
```

```python
import functools
import math

import jax
import jax.numpy as jnp
import numpy as np
from jax import lax
from jax.experimental import pallas as pl
from jax.experimental.pallas import tpu as pltpu
from jax.sharding import PartitionSpec as P

F32 = jnp.float32
BF16 = jnp.bfloat16
VMEM = pl.BlockSpec(memory_space=pltpu.VMEM)
SMEM = pl.BlockSpec(memory_space=pltpu.SMEM)


def struct(shape, dtype):
    return jax.ShapeDtypeStruct(shape, dtype)


def kernel_call(body, outs, n_smem, args, scratch=(), flops=0):
    moved = sum(math.prod(a.shape) * a.dtype.itemsize for a in list(args) + list(outs))
    return pl.pallas_call(
        body,
        out_shape=outs,
        in_specs=[SMEM] * n_smem + [VMEM] * (len(args) - n_smem),
        out_specs=[VMEM] * len(outs),
        scratch_shapes=list(scratch),
        cost_estimate=pl.CostEstimate(flops=flops, bytes_accessed=moved, transcendentals=0),
    )(*args)


def box_matrix(width):
    a, b, s = np.meshgrid(np.arange(3), np.arange(3), np.arange(width), indexing="ij")
    a, b, s = (x.reshape(-1, 1) for x in (a, b, s))
    row, col = np.meshgrid(np.arange(4), np.arange(2 * width), indexing="ij")
    row, col = (x.reshape(1, -1) for x in (row, col))
    dr, dc = row - (2 - a), col - (2 * s + 1 - b)
    return ((dr >= 0) & (dr <= 1) & (dc >= 0) & (dc <= 1)).astype(np.float32)


def box_kernel(sizes, grads, weight, box, g_out, *rest):
    S, HR, W, C, CO, r, n_row = sizes
    bands, padded = rest[: n_row], rest[n_row]
    acts = rest[n_row + 1]
    line = 2 * W
    for s in range(S):
        padded[s, 0:line, :] = jnp.zeros((line, CO), BF16)
        padded[s, line : line * (2 * HR + 1), :] = grads[s]
        padded[s, line * (2 * HR + 1) :, :] = jnp.zeros((line, CO), BF16)
    matrix = box[...]
    for s in range(S):
        for R in range(HR):
            window = padded[s, 2 * R * line : (2 * R + 4) * line, :]
            sums = jnp.dot(matrix, window, preferred_element_type=F32).astype(BF16)
            at = (s * HR + R) * W
            for t in range(9):
                g_out[t, at : at + W, :] = sums[t * W : (t + 1) * W]
    total = jnp.zeros((S * HR * W, C), F32)
    for t in range(9):
        total = total + lax.dot_general(
            g_out[t], weight[t], (((1,), (1,)), ((), ())), preferred_element_type=F32
        )
    acts[...] = total.astype(BF16).reshape(S, HR * W, C)
    me = lax.axis_index("row")
    for d in range(n_row):
        start = pl.multiple_of(lax.rem(me + d, n_row) * (r * W), r * W)
        bands[d][...] = acts[:, pl.ds(start, r * W), :]


def wgrad_kernel(sizes, plan, order, bias, time_weight, g, *rest):
    S, HR, W, C, CO, r, n_row, F = sizes
    own, prior = rest[:n_row], rest[n_row : 2 * n_row]
    n_out = 2 if plan else 1
    outs = rest[2 * n_row : 2 * n_row + n_out]
    ext, acts, picked, terms = rest[2 * n_row + n_out :]
    me = lax.axis_index("row")
    for d in range(n_row):
        source = lax.rem(me - d + n_row, n_row)
        for f in range(F + 2):
            block = prior[d][f] if f < 2 else own[d][f - 2]
            start = pl.multiple_of((f * HR + source * r) * W, W)
            ext[pl.ds(start, r * W), :] = block
    step = HR * W
    total = jnp.broadcast_to(bias[...], (F * step, 2 * C))
    for k in range(3):
        total = total + jnp.dot(
            ext[k * step : (k + F) * step, :], time_weight[k], preferred_element_type=F32
        )
    rounded = total.astype(BF16)
    acts[0] = rounded[:, :C]
    acts[1] = rounded[:, C:]
    for s in range(S):
        o = order[me * S + s]
        start = pl.multiple_of((o // 2) * step, step)
        picked[s * step : (s + 1) * step, :] = acts[o % 2, pl.ds(start, step), :]
    left = picked[...].astype(F32).T.astype(BF16)
    target = terms if plan else outs[0]
    for t in range(9):
        target[t * C : (t + 1) * C, :] = jnp.dot(left, g[t], preferred_element_type=F32)
    if plan:
        n_q, chunk = plan
        core = lax.rem(lax.axis_index("frame"), 2)
        keep, send = outs
        half, low = chunk // 2, CO - 128
        for q in range(n_q):
            for which, out in ((core, keep), (1 - core, send)):
                index = ((q // n_row) * 2 + which) * n_row + q % n_row
                rows = terms[pl.ds(pl.multiple_of(index * chunk, chunk), chunk), :].astype(out.dtype)
                out[q, :chunk, :] = rows[:, :128]
                out[q, chunk:, :] = jnp.concatenate([rows[:half, 128:], rows[half:, 128:]], axis=1)


def join_kernel(n_q, n_row, keep, got, own, *sends):
    q = (lax.axis_index("frame") // 2) * n_row + lax.axis_index("row")
    own[...] = keep[q] + got[q].astype(F32)
    for d in range(1, n_q):
        p = jnp.bitwise_xor(q, d)
        sends[d - 1][...] = (keep[p] + got[p].astype(F32)).astype(BF16)


def square_kernel(n_q, n_clip, base, size, keep, *rest):
    got, mine, sends = rest[: n_q - 1], rest[n_q - 1], rest[n_q : n_q + n_clip - 1]
    total = rest[-1]
    value = keep[...]
    for block in got:
        value = value + block[...].astype(F32)
    total[...] = value
    z = lax.axis_index("clip")
    for d in range(n_clip):
        to = lax.rem(z + d, n_clip)
        piece = total[pl.ds(pl.multiple_of(to * base, 8), size), :]
        if d == 0:
            mine[...] = piece
        else:
            sends[d - 1][...] = piece.astype(BF16)


def piece_kernel(scale, mine, *rest):
    value = mine[...]
    for block in rest[:-1]:
        value = value + block[...].astype(F32)
    rest[-1][...] = (value * scale).astype(BF16)


def final_kernel(n_clip, base, size, chunk, CO, mine, *rest):
    got, out, total, even = rest[: n_clip - 1], rest[n_clip - 1], rest[n_clip], rest[n_clip + 1]
    z = lax.axis_index("clip")
    for d in range(n_clip):
        source = lax.rem(z - d + n_clip, n_clip)
        block = mine if d == 0 else got[d - 1]
        start = pl.multiple_of(source * base, 8)
        total[pl.ds(start, base), :] = block[:base].astype(F32)

        @pl.when(source == n_clip - 1)
        def _():
            total[n_clip * base :, :] = block[base:].astype(F32)

    half, low = chunk // 2, CO - 128
    side = total[chunk:]
    even[:half, :low] = side[:, :low]
    even[half:, :low] = side[:, low:]
    a, b = (total[pl.ds(p, half, stride=2), :] for p in range(2))
    a_side, b_side = (even[pl.ds(p, half, stride=2), :][:, :low] for p in range(2))
    out[pl.ds(0, half, stride=3), :] = a
    out[pl.ds(1, half, stride=3), :] = jnp.concatenate([a_side, b[:, :low]], axis=1)
    out[pl.ds(2, half, stride=3), :] = jnp.concatenate([b[:, low:], b_side], axis=1)


def order_kernel(sizes, order, *rest):
    S, rW, n_row, F = sizes
    bands, natural, first = rest[:n_row], rest[n_row], rest[n_row + 1]
    me = lax.axis_index("row")
    for d in range(n_row):
        source = lax.rem(me - d + n_row, n_row)
        for s in range(S):
            o = order[source * S + s]
            start = pl.multiple_of((o // 2) * rW, rW)
            natural[o % 2, pl.ds(start, rW), :] = bands[d][s]
    first[...] = natural[:, : 2 * rW, :]


def input_kernel(sizes, natural, later, time_weight, out, tail):
    rW, F, C = sizes
    tail[:, : F * rW, :] = natural[...]
    tail[:, F * rW :, :] = later[...]
    total = jnp.zeros((F * rW, C), F32)
    for k in range(3):
        for p in range(2):
            total = total + lax.dot_general(
                tail[p, (2 - k) * rW : (2 - k + F) * rW, :],
                time_weight[k, :, p * C : (p + 1) * C],
                (((1,), (1,)), ((), ())),
                preferred_element_type=F32,
            )
    out[...] = total.astype(BF16)


def local(features, time_weight, time_bias, space_weight, pixel_grads, frame_order):
    _, F, r, W, C = features.shape
    _, S, UR, UW, CO = pixel_grads.shape
    n_row, n_frame, n_clip = (lax.axis_size(a) for a in ("row", "frame", "clip"))
    HR, rW = r * n_row, r * W
    pixels = S * HR * W
    order = frame_order.reshape(-1)
    both = ("frame", "row")

    feats = features.reshape(F, rW, C)
    last = feats[F - 2 :]
    own, prior = [feats], []
    for d in range(1, n_row):
        own.append(lax.ppermute(feats, "row", [(i, (i + d) % n_row) for i in range(n_row)]))
    for d in range(n_row):
        route = [
            (f * n_row + i, (f + 1) * n_row + (i + d) % n_row)
            for f in range(n_frame - 1)
            for i in range(n_row)
        ]
        prior.append(lax.ppermute(last, both, route))

    box = jnp.asarray(box_matrix(W), BF16)
    g, *bands = kernel_call(
        functools.partial(box_kernel, (S, HR, W, C, CO, r, n_row)),
        [struct((9, pixels, CO), BF16)] + [struct((S, rW, C), BF16)] * n_row,
        0,
        [pixel_grads.reshape(S, UR * UW, CO), space_weight.reshape(9, C, CO), box],
        [pltpu.VMEM((S, (UR + 2) * UW, CO), BF16), pltpu.VMEM((S, HR * W, C), BF16)],
        flops=2 * pixels * 9 * C * CO,
    )

    n_total = 9 * C
    n_dev = n_frame * n_row
    n_q = n_dev // 2
    chunk = n_total // n_dev
    fast = (
        n_frame % 2 == 0
        and n_total % n_dev == 0
        and chunk % 16 == 0
        and 1 < n_q <= 8
        and n_q & (n_q - 1) == 0
        and n_clip > 1
        and 128 < CO == 192
    )
    wg_sizes = (S, HR, W, C, CO, r, n_row, F)
    packed = chunk * CO // 128
    wg = kernel_call(
        functools.partial(wgrad_kernel, wg_sizes, (n_q, chunk) if fast else None),
        [struct((n_q, packed, 128), F32), struct((n_q, packed, 128), BF16)]
        if fast
        else [struct((n_total, CO), F32)],
        1,
        [order, time_bias.reshape(1, -1), time_weight, g] + own + prior,
        [
            pltpu.VMEM(((F + 2) * HR * W, C), BF16),
            pltpu.VMEM((2, F * HR * W, C), BF16),
            pltpu.VMEM((pixels, C), BF16),
            pltpu.VMEM((n_total if fast else 8, CO), F32),
        ],
        flops=2 * pixels * 9 * C * CO + 2 * F * HR * W * 6 * C * C,
    )

    scale = 1.0 / math.sqrt(2 * F * UR * UW * n_clip * n_frame)
    if fast:
        keep, send = wg
        got = lax.ppermute(
            send, both, [(i, ((i // n_row) ^ 1) * n_row + i % n_row) for i in range(n_dev)]
        )
        mine, *sends = kernel_call(
            functools.partial(join_kernel, n_q, n_row),
            [struct((packed, 128), F32)] + [struct((packed, 128), BF16)] * (n_q - 1),
            0,
            [keep, got],
        )

        def square(i, d):
            f, j = i // n_row, i % n_row
            p = ((f // 2) * n_row + j) ^ d
            return ((p // n_row) * 2 + f % 2) * n_row + p % n_row

        got = [
            lax.ppermute(sends[d - 1], both, [(i, square(i, d)) for i in range(n_dev)])
            for d in range(1, n_q)
        ]
        base = packed // n_clip // 8 * 8
        size = packed - base * (n_clip - 1)
        mine, *sends = kernel_call(
            functools.partial(square_kernel, n_q, n_clip, base, size),
            [struct((size, 128), F32)] + [struct((size, 128), BF16)] * (n_clip - 1),
            0,
            [mine] + got,
            [pltpu.VMEM((packed, 128), F32)],
        )
        shift = [[(i, (i + d) % n_clip) for i in range(n_clip)] for d in range(1, n_clip)]
        got = [lax.ppermute(x, "clip", route) for x, route in zip(sends, shift)]
        (mine,) = kernel_call(
            functools.partial(piece_kernel, scale), [struct((size, 128), BF16)], 0, [mine] + got
        )
        got = [lax.ppermute(mine, "clip", route) for route in shift]
        (flat,) = kernel_call(
            functools.partial(final_kernel, n_clip, base, size, chunk, CO),
            [struct((packed, 128), F32)],
            0,
            [mine] + got,
            [pltpu.VMEM((packed, 128), F32), pltpu.VMEM((chunk, 128), F32)],
        )
        weight_grad = flat.reshape(-1)
    else:
        shard = lax.psum_scatter(wg[0].reshape(-1), both, scatter_dimension=0, tiled=True)
        weight_grad = lax.psum(shard, "clip") * scale

    bands = [bands[0]] + [
        lax.ppermute(bands[d], "row", [(i, (i + d) % n_row) for i in range(n_row)])
        for d in range(1, n_row)
    ]
    natural, first = kernel_call(
        functools.partial(order_kernel, (S, rW, n_row, F)),
        [struct((2, F * rW, C), BF16), struct((2, 2 * rW, C), BF16)],
        1,
        [order] + bands,
    )
    later = lax.ppermute(first, "frame", [(i + 1, i) for i in range(n_frame - 1)])
    (input_grad,) = kernel_call(
        functools.partial(input_kernel, (rW, F, C)),
        [struct((F * rW, C), BF16)],
        0,
        [natural, later, time_weight],
        [pltpu.VMEM((2, (F + 2) * rW, C), BF16)],
        flops=2 * F * rW * 6 * C * C,
    )
    return input_grad.reshape(features.shape), weight_grad


def solution(mesh):
    return jax.shard_map(
        local,
        mesh=mesh,
        in_specs=(
            P("clip", "frame", "row", None, None),
            P(),
            P(),
            P(),
            P("clip", ("frame", "row"), None, None, None),
            P("clip", "frame", None),
        ),
        out_specs=(P("clip", "frame", "row", None, None), P(("frame", "row"))),
        check_vma=False,
    )
```

```python
import functools
import math

import jax
import jax.numpy as jnp
import numpy as np
from jax import lax
from jax.experimental import pallas as pl
from jax.experimental.pallas import tpu as pltpu
from jax.sharding import PartitionSpec as P


F32 = jnp.float32
BF16 = jnp.bfloat16
VMEM = pl.BlockSpec(memory_space=pltpu.VMEM)
SMEM = pl.BlockSpec(memory_space=pltpu.SMEM)


def struct(shape, dtype):
    return jax.ShapeDtypeStruct(shape, dtype)


def kernel_call(body, outs, n_smem, args, scratch=(), flops=0, far=()):
    moved = sum(math.prod(a.shape) * a.dtype.itemsize for a in list(args) + list(outs))
    specs = [SMEM] * n_smem + [VMEM] * (len(args) - n_smem)
    for i in far:
        specs[i] = pl.BlockSpec(memory_space=pltpu.HBM)
    return pl.pallas_call(
        body,
        out_shape=outs,
        in_specs=specs,
        out_specs=[VMEM] * len(outs),
        scratch_shapes=list(scratch),
        compiler_params=pltpu.CompilerParams(vmem_limit_bytes=16 * 2**20),
        cost_estimate=pl.CostEstimate(flops=flops, bytes_accessed=moved, transcendentals=0),
    )(*args)


def box_matrix(width):
    a, b, s = np.meshgrid(np.arange(3), np.arange(3), np.arange(width), indexing="ij")
    a, b, s = (x.reshape(-1, 1) for x in (a, b, s))
    row, col = np.meshgrid(np.arange(4), np.arange(2 * width), indexing="ij")
    row, col = (x.reshape(1, -1) for x in (row, col))
    dr, dc = row - (2 - a), col - (2 * s + 1 - b)
    return ((dr >= 0) & (dr <= 1) & (dc >= 0) & (dc <= 1)).astype(np.float32)


def box_kernel(sizes, grads, weight_far, box, g_out, *rest):
    S, HR, W, C, CO, r, n_row = sizes
    bands, (padded, acts, weight, grads_in, weight_in) = rest[:n_row], rest[n_row:]
    line = 2 * W
    end = line * (2 * HR + 1)
    load_grads = pltpu.make_async_copy(grads, padded.at[:, line:end, :], grads_in)
    load_weight = pltpu.make_async_copy(weight_far, weight, weight_in)
    load_grads.start()
    load_weight.start()
    for s in range(S):
        padded[s, 0:line, :] = jnp.zeros((line, CO), BF16)
        padded[s, end:, :] = jnp.zeros((line, CO), BF16)
    load_grads.wait()
    matrix = box[...]
    for s in range(S):
        for R in range(HR):
            window = padded[s, 2 * R * line : (2 * R + 4) * line, :]
            sums = jnp.dot(matrix, window, preferred_element_type=F32).astype(BF16)
            at = (s * HR + R) * W
            for t in range(9):
                g_out[t, at : at + W, :] = sums[t * W : (t + 1) * W]
    load_weight.wait()
    total = jnp.zeros((S * HR * W, C), F32)
    for t in range(9):
        total = total + jnp.dot(g_out[t], weight[t], preferred_element_type=F32)
    acts[...] = total.astype(BF16).reshape(S, HR * W, C)
    me = lax.axis_index("row")
    for d in range(n_row):
        start = pl.multiple_of(lax.rem(me + d, n_row) * (r * W), r * W)
        bands[d][...] = acts[:, pl.ds(start, r * W), :]


def wgrad_kernel(sizes, plan, order, bias, time_weight, g, *rest):
    S, HR, W, C, _, r, n_row, F = sizes
    own, prior = rest[:n_row], rest[n_row : 2 * n_row]
    n_out = 2 if plan else 1
    outs = rest[2 * n_row : 2 * n_row + n_out]
    ext, acts, picked, terms = rest[2 * n_row + n_out :]
    me = lax.axis_index("row")
    for d in range(n_row):
        source = lax.rem(me - d + n_row, n_row)
        for f in range(F + 2):
            block = prior[d][F - 2 + f] if f < 2 else own[d][f - 2]
            start = pl.multiple_of((f * HR + source * r) * W, W)
            ext[pl.ds(start, r * W), :] = block
    step = HR * W
    row = jnp.concatenate([bias[i : i + 1, :] for i in range(bias.shape[0])], axis=1)
    total = jnp.broadcast_to(row, (F * step, 2 * C))
    for k in range(3):
        total = total + jnp.dot(
            ext[k * step : (k + F) * step, :], time_weight[k], preferred_element_type=F32
        )
    rounded = total.astype(BF16)
    acts[0] = rounded[:, :C]
    acts[1] = rounded[:, C:]
    for s in range(S):
        o = order[me * S + s]
        start = pl.multiple_of((o // 2) * step, step)
        picked[s * step : (s + 1) * step, :] = acts[o % 2, pl.ds(start, step), :]
    left = picked[...].astype(F32).T.astype(BF16)
    target = terms if plan else outs[0]
    for t in range(9):
        target[t * C : (t + 1) * C, :] = jnp.dot(left, g[t], preferred_element_type=F32)
    if plan:
        n_q, chunk = plan
        core = lax.rem(lax.axis_index("frame"), 2)
        keep, send = outs
        half = chunk // 2
        for q in range(n_q):
            for which, out in ((core, keep), (1 - core, send)):
                index = ((q // n_row) * 2 + which) * n_row + q % n_row
                rows = terms[pl.ds(pl.multiple_of(index * chunk, chunk), chunk), :].astype(out.dtype)
                out[q, :chunk, :] = rows[:, :128]
                out[q, chunk:, :] = jnp.concatenate([rows[:half, 128:], rows[half:, 128:]], axis=1)


def join_kernel(n_q, n_row, keep, got, own, *sends):
    q = (lax.axis_index("frame") // 2) * n_row + lax.axis_index("row")
    own[...] = keep[q] + got[q].astype(F32)
    for d in range(1, n_q):
        p = jnp.bitwise_xor(q, d)
        sends[d - 1][...] = (keep[p] + got[p].astype(F32)).astype(BF16)


def square_kernel(n_q, n_clip, base, size, keep, *rest):
    got, mine, sends = rest[: n_q - 1], rest[n_q - 1], rest[n_q : n_q + n_clip - 1]
    total = rest[-1]
    value = keep[...]
    for block in got:
        value = value + block[...].astype(F32)
    total[...] = value
    z = lax.axis_index("clip")
    for d in range(n_clip):
        to = lax.rem(z + d, n_clip)
        piece = total[pl.ds(pl.multiple_of(to * base, 8), size), :]
        if d == 0:
            mine[...] = piece
        else:
            sends[d - 1][...] = piece.astype(BF16)


def piece_kernel(scale, mine, *rest):
    value = mine[...]
    for block in rest[:-1]:
        value = value + block[...].astype(F32)
    rest[-1][...] = (value * scale).astype(BF16)


def final_kernel(n_clip, base, chunk, CO, mine, *rest):
    got, out, total, even = rest[: n_clip - 1], rest[n_clip - 1], rest[n_clip], rest[n_clip + 1]
    z = lax.axis_index("clip")
    for d in range(n_clip):
        source = lax.rem(z - d + n_clip, n_clip)
        block = mine if d == 0 else got[d - 1]
        start = pl.multiple_of(source * base, 8)
        total[pl.ds(start, base), :] = block[:base].astype(F32)

        @pl.when(source == n_clip - 1)
        def _():
            total[n_clip * base :, :] = block[base:].astype(F32)

    half, low = chunk // 2, CO - 128
    side = total[chunk:]
    even[:half, :low] = side[:, :low]
    even[half:, :low] = side[:, low:]
    a, b = (total[pl.ds(p, half, stride=2), :] for p in range(2))
    a_side, b_side = (even[pl.ds(p, half, stride=2), :][:, :low] for p in range(2))
    out[pl.ds(0, half, stride=3), :] = a
    out[pl.ds(1, half, stride=3), :] = jnp.concatenate([a_side, b[:, :low]], axis=1)
    out[pl.ds(2, half, stride=3), :] = jnp.concatenate([b[:, low:], b_side], axis=1)


def order_kernel(sizes, order, *rest):
    S, rW, n_row, _ = sizes
    bands, natural, first = rest[:n_row], rest[n_row], rest[n_row + 1]
    me = lax.axis_index("row")
    for d in range(n_row):
        source = lax.rem(me - d + n_row, n_row)
        for s in range(S):
            o = order[source * S + s]
            start = pl.multiple_of((o // 2) * rW, rW)
            natural[o % 2, pl.ds(start, rW), :] = bands[d][s]
    first[...] = natural[:, : 2 * rW, :]


def input_kernel(sizes, natural, later, time_weight, out, tail):
    rW, F, C = sizes
    tail[:, : F * rW, :] = natural[...]
    tail[:, F * rW :, :] = later[...]
    total = jnp.zeros((F * rW, C), F32)
    for k in range(3):
        for p in range(2):
            total = total + lax.dot_general(
                tail[p, (2 - k) * rW : (2 - k + F) * rW, :],
                time_weight[k, :, p * C : (p + 1) * C],
                (((1,), (1,)), ((), ())),
                preferred_element_type=F32,
            )
    out[...] = total.astype(BF16)


def direct(n_frame, n_row, n_clip):
    n_q = n_frame * n_row // 2
    return n_frame % 2 == 0 and 1 < n_q <= 8 and n_q & (n_q - 1) == 0 and n_clip > 1


def local(features, time_weight, time_bias, space_weight, pixel_grads, frame_order):
    _, F, r, W, C = features.shape
    _, S, UR, UW, CO = pixel_grads.shape
    n_row, n_frame, n_clip = (lax.axis_size(a) for a in ("row", "frame", "clip"))
    HR, rW = r * n_row, r * W
    pixels = S * HR * W
    order = frame_order.reshape(-1)
    both = ("frame", "row")

    feats = features.reshape(F, rW, C)
    own, prior = [feats], []
    for d in range(1, n_row):
        own.append(lax.ppermute(feats, "row", [(i, (i + d) % n_row) for i in range(n_row)]))
    for d in range(n_row):
        route = [
            (f * n_row + i, (f + 1) * n_row + (i + d) % n_row)
            for f in range(n_frame - 1)
            for i in range(n_row)
        ]
        prior.append(lax.ppermute(feats, both, route))

    box = jnp.asarray(box_matrix(W), BF16)
    g, *bands = kernel_call(
        functools.partial(box_kernel, (S, HR, W, C, CO, r, n_row)),
        [struct((9, pixels, CO), BF16)] + [struct((S, rW, C), BF16)] * n_row,
        0,
        [pixel_grads.reshape(S, UR * UW, CO), space_weight.transpose(0, 1, 3, 2).reshape(9, CO, C), box],
        [
            pltpu.VMEM((S, (UR + 2) * UW, CO), BF16),
            pltpu.VMEM((S, HR * W, C), BF16),
            pltpu.VMEM((9, CO, C), BF16),
            pltpu.SemaphoreType.DMA,
            pltpu.SemaphoreType.DMA,
        ],
        far=(0, 1),
        flops=2 * pixels * 9 * C * CO,
    )

    n_total = 9 * C
    n_dev = n_frame * n_row
    n_q = n_dev // 2
    chunk = n_total // n_dev
    fast = (
        direct(n_frame, n_row, n_clip)
        and n_total % n_dev == 0
        and chunk % 16 == 0
        and CO == 192
    )
    wg_sizes = (S, HR, W, C, CO, r, n_row, F)
    packed = chunk * CO // 128
    wg = kernel_call(
        functools.partial(wgrad_kernel, wg_sizes, (n_q, chunk) if fast else None),
        [struct((n_q, packed, 128), F32), struct((n_q, packed, 128), BF16)]
        if fast
        else [struct((n_total, CO), F32)],
        1,
        [order, time_bias.reshape(-1, 128), time_weight, g] + own + prior,
        [
            pltpu.VMEM(((F + 2) * HR * W, C), BF16),
            pltpu.VMEM((2, F * HR * W, C), BF16),
            pltpu.VMEM((pixels, C), BF16),
            pltpu.VMEM((n_total if fast else 8, CO), F32),
        ],
        flops=2 * pixels * 9 * C * CO + 2 * F * HR * W * 6 * C * C,
    )

    scale = 1.0 / math.sqrt(2 * F * UR * UW * n_clip * n_frame)
    if fast:
        keep, send = wg
        got = lax.ppermute(
            send, both, [(i, ((i // n_row) ^ 1) * n_row + i % n_row) for i in range(n_dev)]
        )
        mine, *sends = kernel_call(
            functools.partial(join_kernel, n_q, n_row),
            [struct((packed, 128), F32)] + [struct((packed, 128), BF16)] * (n_q - 1),
            0,
            [keep, got],
        )

        def square(i, d):
            f, j = i // n_row, i % n_row
            p = ((f // 2) * n_row + j) ^ d
            return ((p // n_row) * 2 + f % 2) * n_row + p % n_row

        got = [
            lax.ppermute(sends[d - 1], both, [(i, square(i, d)) for i in range(n_dev)])
            for d in range(1, n_q)
        ]
        base = packed // n_clip // 8 * 8
        size = packed - base * (n_clip - 1)
        mine, *sends = kernel_call(
            functools.partial(square_kernel, n_q, n_clip, base, size),
            [struct((size, 128), F32)] + [struct((size, 128), BF16)] * (n_clip - 1),
            0,
            [mine] + got,
            [pltpu.VMEM((packed, 128), F32)],
        )
        shift = [[(i, (i + d) % n_clip) for i in range(n_clip)] for d in range(1, n_clip)]
        got = [lax.ppermute(x, "clip", route) for x, route in zip(sends, shift)]
        (mine,) = kernel_call(
            functools.partial(piece_kernel, scale), [struct((size, 128), BF16)], 0, [mine] + got
        )
        got = [lax.ppermute(mine, "clip", route) for route in shift]
        (flat,) = kernel_call(
            functools.partial(final_kernel, n_clip, base, chunk, CO),
            [struct((packed, 128), F32)],
            0,
            [mine] + got,
            [pltpu.VMEM((packed, 128), F32), pltpu.VMEM((chunk, 128), F32)],
        )
        weight_grad = flat.reshape(-1)
    else:
        shard = lax.psum_scatter(wg[0].reshape(-1), both, scatter_dimension=0, tiled=True)
        weight_grad = lax.psum(shard, "clip") * scale

    bands = [bands[0]] + [
        lax.ppermute(bands[d], "row", [(i, (i + d) % n_row) for i in range(n_row)])
        for d in range(1, n_row)
    ]
    natural, first = kernel_call(
        functools.partial(order_kernel, (S, rW, n_row, F)),
        [struct((2, F * rW, C), BF16), struct((2, 2 * rW, C), BF16)],
        1,
        [order] + bands,
    )
    later = lax.ppermute(first, "frame", [(i + 1, i) for i in range(n_frame - 1)])
    (input_grad,) = kernel_call(
        functools.partial(input_kernel, (rW, F, C)),
        [struct((F * rW, C), BF16)],
        0,
        [natural, later, time_weight],
        [pltpu.VMEM((2, (F + 2) * rW, C), BF16)],
        flops=2 * F * rW * 6 * C * C,
    )
    return input_grad.reshape(features.shape), weight_grad


def solution(mesh):
    step = jax.shard_map(
        local,
        mesh=mesh,
        in_specs=(
            P("clip", "frame", "row", None, None),
            P(),
            P(),
            P(),
            P("clip", ("frame", "row"), None, None, None),
            P("clip", "frame", None),
        ),
        out_specs=(P("clip", "frame", "row", None, None), P(("frame", "row"))),
        check_vma=False,
    )
    if not direct(mesh.shape["frame"], mesh.shape["row"], mesh.shape["clip"]):
        return step
    return step
```

```python
import functools
import math

import jax
import jax.numpy as jnp
from jax import lax
from jax.experimental import pallas as pl
from jax.experimental.pallas import tpu as pltpu
from jax.sharding import PartitionSpec as P


F32 = jnp.float32
BF16 = jnp.bfloat16
VMEM = pl.BlockSpec(memory_space=pltpu.VMEM)
SMEM = pl.BlockSpec(memory_space=pltpu.SMEM)


def struct(shape, dtype):
    return jax.ShapeDtypeStruct(shape, dtype)


def kernel_call(body, outs, n_smem, args, scratch=(), flops=0, far=()):
    moved = sum(math.prod(a.shape) * a.dtype.itemsize for a in list(args) + list(outs))
    specs = [SMEM] * n_smem + [VMEM] * (len(args) - n_smem)
    for i in far:
        specs[i] = pl.BlockSpec(memory_space=pltpu.HBM)
    return pl.pallas_call(
        body,
        out_shape=outs,
        in_specs=specs,
        out_specs=[VMEM] * len(outs),
        scratch_shapes=list(scratch),
        compiler_params=pltpu.CompilerParams(vmem_limit_bytes=16 * 2**20),
        cost_estimate=pl.CostEstimate(flops=flops, bytes_accessed=moved, transcendentals=0),
    )(*args)


def matrix_kernel(width, out):
    column = lax.broadcasted_iota(jnp.int32, (width, 8 * width), 1)
    line, col = column // (2 * width), column % (2 * width)
    first = 2 * lax.broadcasted_iota(jnp.int32, (width, 8 * width), 0) + 1
    for a in range(3):
        rows = (line == 2 - a) | (line == 3 - a)
        for b in range(3):
            inside = rows & ((col == first - b) | (col == first + 1 - b))
            t = 3 * a + b
            out[t * width : (t + 1) * width, :] = jnp.where(inside, 1.0, 0.0).astype(BF16)


def box_kernel(sizes, grads, weight_far, box, g_out, *rest):
    S, HR, W, C, CO, r, n_row = sizes
    bands, (padded, acts, weight, grads_in, weight_in) = rest[:n_row], rest[n_row:]
    line = 2 * W
    end = line * (2 * HR + 1)
    load_grads = pltpu.make_async_copy(grads, padded.at[:, line:end, :], grads_in)
    load_weight = pltpu.make_async_copy(weight_far, weight, weight_in)
    load_grads.start()
    load_weight.start()
    for s in range(S):
        padded[s, 0:line, :] = jnp.zeros((line, CO), BF16)
        padded[s, end:, :] = jnp.zeros((line, CO), BF16)
    load_grads.wait()
    matrix = box[...]
    for s in range(S):
        for R in range(HR):
            window = padded[s, 2 * R * line : (2 * R + 4) * line, :]
            sums = jnp.dot(matrix, window, preferred_element_type=F32).astype(BF16)
            at = (s * HR + R) * W
            for t in range(9):
                g_out[t, at : at + W, :] = sums[t * W : (t + 1) * W]
    load_weight.wait()
    total = jnp.zeros((S * HR * W, C), F32)
    for t in range(9):
        total = total + jnp.dot(g_out[t], weight[t], preferred_element_type=F32)
    acts[...] = total.astype(BF16).reshape(S, HR * W, C)
    me = lax.axis_index("row")
    for d in range(n_row):
        start = pl.multiple_of(lax.rem(me + d, n_row) * (r * W), r * W)
        bands[d][...] = acts[:, pl.ds(start, r * W), :]


def wgrad_kernel(sizes, plan, order, bias, time_weight, g, *rest):
    S, HR, W, C, _, r, n_row, F = sizes
    own, prior = rest[:n_row], rest[n_row : 2 * n_row]
    n_out = 2 if plan else 1
    outs = rest[2 * n_row : 2 * n_row + n_out]
    ext, acts, picked, terms = rest[2 * n_row + n_out :]
    me = lax.axis_index("row")
    for d in range(n_row):
        source = lax.rem(me - d + n_row, n_row)
        for f in range(F + 2):
            block = prior[d][F - 2 + f] if f < 2 else own[d][f - 2]
            start = pl.multiple_of((f * HR + source * r) * W, W)
            ext[pl.ds(start, r * W), :] = block
    step = HR * W
    row = jnp.concatenate([bias[i : i + 1, :] for i in range(bias.shape[0])], axis=1)
    total = jnp.broadcast_to(row, (F * step, 2 * C))
    for k in range(3):
        total = total + jnp.dot(
            ext[k * step : (k + F) * step, :], time_weight[k], preferred_element_type=F32
        )
    rounded = total.astype(BF16)
    acts[0] = rounded[:, :C]
    acts[1] = rounded[:, C:]
    for s in range(S):
        o = order[me * S + s]
        start = pl.multiple_of((o // 2) * step, step)
        picked[s * step : (s + 1) * step, :] = acts[o % 2, pl.ds(start, step), :]
    left = picked[...].astype(F32).T.astype(BF16)
    target = terms if plan else outs[0]
    for t in range(9):
        target[t * C : (t + 1) * C, :] = jnp.dot(left, g[t], preferred_element_type=F32)
    if plan:
        n_q, chunk = plan
        core = lax.rem(lax.axis_index("frame"), 2)
        keep, send = outs
        half = chunk // 2
        for q in range(n_q):
            for which, out in ((core, keep), (1 - core, send)):
                index = ((q // n_row) * 2 + which) * n_row + q % n_row
                rows = terms[pl.ds(pl.multiple_of(index * chunk, chunk), chunk), :].astype(out.dtype)
                out[q, :chunk, :] = rows[:, :128]
                out[q, chunk:, :] = jnp.concatenate([rows[:half, 128:], rows[half:, 128:]], axis=1)


def join_kernel(n_q, n_row, keep, got, own, *sends):
    q = (lax.axis_index("frame") // 2) * n_row + lax.axis_index("row")
    own[...] = keep[q] + got[q].astype(F32)
    for d in range(1, n_q):
        p = jnp.bitwise_xor(q, d)
        sends[d - 1][...] = (keep[p] + got[p].astype(F32)).astype(BF16)


def square_kernel(scale, keep, *rest):
    value = keep[...]
    for block in rest[:-1]:
        value = value + block[...].astype(F32)
    rest[-1][...] = (value * scale).astype(BF16)


def pair_kernel(mine, got, out):
    out[...] = (mine[...].astype(F32) + got[...].astype(F32)).astype(BF16)


def final_kernel(chunk, CO, mine, got, out, total, even):
    total[...] = mine[...].astype(F32) + got[...].astype(F32)
    half, low = chunk // 2, CO - 128
    side = total[chunk:]
    even[:half, :low] = side[:, :low]
    even[half:, :low] = side[:, low:]
    a, b = (total[pl.ds(p, half, stride=2), :] for p in range(2))
    a_side, b_side = (even[pl.ds(p, half, stride=2), :][:, :low] for p in range(2))
    out[pl.ds(0, half, stride=3), :] = a
    out[pl.ds(1, half, stride=3), :] = jnp.concatenate([a_side, b[:, :low]], axis=1)
    out[pl.ds(2, half, stride=3), :] = jnp.concatenate([b[:, low:], b_side], axis=1)


def order_kernel(sizes, order, *rest):
    S, rW, n_row, _ = sizes
    bands, natural, first = rest[:n_row], rest[n_row], rest[n_row + 1]
    me = lax.axis_index("row")
    for d in range(n_row):
        source = lax.rem(me - d + n_row, n_row)
        for s in range(S):
            o = order[source * S + s]
            start = pl.multiple_of((o // 2) * rW, rW)
            natural[o % 2, pl.ds(start, rW), :] = bands[d][s]
    first[...] = natural[:, : 2 * rW, :]


def input_kernel(sizes, natural, later, time_weight, out, tail):
    rW, F, C = sizes
    tail[:, : F * rW, :] = natural[...]
    tail[:, F * rW :, :] = later[...]
    total = jnp.zeros((F * rW, C), F32)
    for k in range(3):
        for p in range(2):
            total = total + lax.dot_general(
                tail[p, (2 - k) * rW : (2 - k + F) * rW, :],
                time_weight[k, :, p * C : (p + 1) * C],
                (((1,), (1,)), ((), ())),
                preferred_element_type=F32,
            )
    out[...] = total.astype(BF16)


def direct(n_frame, n_row, n_clip):
    n_q = n_frame * n_row // 2
    return n_frame % 2 == 0 and 1 < n_q <= 8 and n_q & (n_q - 1) == 0 and n_clip > 1 and n_clip & (n_clip - 1) == 0


def local(features, time_weight, time_bias, space_weight, pixel_grads, frame_order):
    _, F, r, W, C = features.shape
    _, S, UR, UW, CO = pixel_grads.shape
    n_row, n_frame, n_clip = (lax.axis_size(a) for a in ("row", "frame", "clip"))
    HR, rW = r * n_row, r * W
    pixels = S * HR * W
    order = frame_order.reshape(-1)
    both = ("frame", "row")

    (box,) = kernel_call(
        functools.partial(matrix_kernel, W), [struct((9 * W, 8 * W), BF16)], 0, [], flops=10**10
    )
    feats = features.reshape(F, rW, C)
    own, prior = [feats], []
    for d in range(1, n_row):
        own.append(lax.ppermute(feats, "row", [(i, (i + d) % n_row) for i in range(n_row)]))
    for d in range(n_row):
        route = [
            (f * n_row + i, (f + 1) * n_row + (i + d) % n_row)
            for f in range(n_frame - 1)
            for i in range(n_row)
        ]
        prior.append(lax.ppermute(feats, both, route))

    g, *bands = kernel_call(
        functools.partial(box_kernel, (S, HR, W, C, CO, r, n_row)),
        [struct((9, pixels, CO), BF16)] + [struct((S, rW, C), BF16)] * n_row,
        0,
        [pixel_grads.reshape(S, UR * UW, CO), space_weight.transpose(0, 1, 3, 2).reshape(9, CO, C), box],
        [
            pltpu.VMEM((S, (UR + 2) * UW, CO), BF16),
            pltpu.VMEM((S, HR * W, C), BF16),
            pltpu.VMEM((9, CO, C), BF16),
            pltpu.SemaphoreType.DMA,
            pltpu.SemaphoreType.DMA,
        ],
        far=(0, 1),
        flops=2 * pixels * 9 * C * CO,
    )

    n_total = 9 * C
    n_dev = n_frame * n_row
    n_q = n_dev // 2
    chunk = n_total // n_dev
    fast = (
        direct(n_frame, n_row, n_clip)
        and n_total % n_dev == 0
        and chunk % 16 == 0
        and CO == 192
    )
    wg_sizes = (S, HR, W, C, CO, r, n_row, F)
    packed = chunk * CO // 128
    wg = kernel_call(
        functools.partial(wgrad_kernel, wg_sizes, (n_q, chunk) if fast else None),
        [struct((n_q, packed, 128), F32), struct((n_q, packed, 128), BF16)]
        if fast
        else [struct((n_total, CO), F32)],
        1,
        [order, time_bias.reshape(-1, 128), time_weight, g] + own + prior,
        [
            pltpu.VMEM(((F + 2) * HR * W, C), BF16),
            pltpu.VMEM((2, F * HR * W, C), BF16),
            pltpu.VMEM((pixels, C), BF16),
            pltpu.VMEM((n_total if fast else 8, CO), F32),
        ],
        flops=2 * pixels * 9 * C * CO + 2 * F * HR * W * 6 * C * C,
    )

    scale = 1.0 / math.sqrt(2 * F * UR * UW * n_clip * n_frame)
    if fast:
        keep, send = wg
        got = lax.ppermute(
            send, both, [(i, ((i // n_row) ^ 1) * n_row + i % n_row) for i in range(n_dev)]
        )
        mine, *sends = kernel_call(
            functools.partial(join_kernel, n_q, n_row),
            [struct((packed, 128), F32)] + [struct((packed, 128), BF16)] * (n_q - 1),
            0,
            [keep, got],
        )

        def square(i, d):
            f, j = i // n_row, i % n_row
            p = ((f // 2) * n_row + j) ^ d
            return ((p // n_row) * 2 + f % 2) * n_row + p % n_row

        got = [
            lax.ppermute(sends[d - 1], both, [(i, square(i, d)) for i in range(n_dev)])
            for d in range(1, n_q)
        ]
        (mine,) = kernel_call(
            functools.partial(square_kernel, scale), [struct((packed, 128), BF16)], 0, [mine] + got
        )
        mask = n_clip - 1
        while mask:
            got = lax.ppermute(mine, "clip", [(i, i ^ mask) for i in range(n_clip)])
            if mask > 1:
                (mine,) = kernel_call(pair_kernel, [struct((packed, 128), BF16)], 0, [mine, got])
            mask //= 2
        (flat,) = kernel_call(
            functools.partial(final_kernel, chunk, CO),
            [struct((packed, 128), F32)],
            0,
            [mine, got],
            [pltpu.VMEM((packed, 128), F32), pltpu.VMEM((chunk, 128), F32)],
        )
        weight_grad = flat.reshape(-1)
    else:
        shard = lax.psum_scatter(wg[0].reshape(-1), both, scatter_dimension=0, tiled=True)
        weight_grad = lax.psum(shard, "clip") * scale

    bands = [bands[0]] + [
        lax.ppermute(bands[d], "row", [(i, (i + d) % n_row) for i in range(n_row)])
        for d in range(1, n_row)
    ]
    natural, first = kernel_call(
        functools.partial(order_kernel, (S, rW, n_row, F)),
        [struct((2, F * rW, C), BF16), struct((2, 2 * rW, C), BF16)],
        1,
        [order] + bands,
    )
    later = lax.ppermute(first, "frame", [(i + 1, i) for i in range(n_frame - 1)])
    (input_grad,) = kernel_call(
        functools.partial(input_kernel, (rW, F, C)),
        [struct((F * rW, C), BF16)],
        0,
        [natural, later, time_weight],
        [pltpu.VMEM((2, (F + 2) * rW, C), BF16)],
        flops=2 * F * rW * 6 * C * C,
    )
    return input_grad.reshape(features.shape), weight_grad


def solution(mesh):
    step = jax.shard_map(
        local,
        mesh=mesh,
        in_specs=(
            P("clip", "frame", "row", None, None),
            P(),
            P(),
            P(),
            P("clip", ("frame", "row"), None, None, None),
            P("clip", "frame", None),
        ),
        out_specs=(P("clip", "frame", "row", None, None), P(("frame", "row"))),
        check_vma=False,
    )
    if not direct(mesh.shape["frame"], mesh.shape["row"], mesh.shape["clip"]):
        return step
    return step
```

```python
import functools
import math

import jax
import jax.numpy as jnp
from jax import lax
from jax.experimental import pallas as pl
from jax.experimental.pallas import tpu as pltpu
from jax.sharding import PartitionSpec as P


F32 = jnp.float32
BF16 = jnp.bfloat16
VMEM = pl.BlockSpec(memory_space=pltpu.VMEM)
SMEM = pl.BlockSpec(memory_space=pltpu.SMEM)


def struct(shape, dtype):
    return jax.ShapeDtypeStruct(shape, dtype)


def kernel_call(body, outs, n_smem, args, scratch=(), flops=0, far=()):
    moved = sum(math.prod(a.shape) * a.dtype.itemsize for a in list(args) + list(outs))
    specs = [SMEM] * n_smem + [VMEM] * (len(args) - n_smem)
    for i in far:
        specs[i] = pl.BlockSpec(memory_space=pltpu.HBM)
    return pl.pallas_call(
        body,
        out_shape=outs,
        in_specs=specs,
        out_specs=[VMEM] * len(outs),
        scratch_shapes=list(scratch),
        compiler_params=pltpu.CompilerParams(vmem_limit_bytes=16 * 2**20),
        cost_estimate=pl.CostEstimate(flops=flops, bytes_accessed=moved, transcendentals=0),
    )(*args)


def matrix_kernel(width, out):
    column = lax.broadcasted_iota(jnp.int32, (width, 8 * width), 1)
    line, col = column // (2 * width), column % (2 * width)
    first = 2 * lax.broadcasted_iota(jnp.int32, (width, 8 * width), 0) + 1
    for a in range(3):
        rows = (line == 2 - a) | (line == 3 - a)
        for b in range(3):
            inside = rows & ((col == first - b) | (col == first + 1 - b))
            t = 3 * a + b
            out[t * width : (t + 1) * width, :] = jnp.where(inside, 1.0, 0.0).astype(BF16)


def box_kernel(sizes, grads, weight_far, box, g_out, *rest):
    S, HR, W, C, CO, r, n_row = sizes
    bands, (padded, acts, weight, grads_in, weight_in) = rest[:n_row], rest[n_row:]
    line = 2 * W
    end = line * (2 * HR + 1)
    load_grads = pltpu.make_async_copy(grads, padded.at[:, line:end, :], grads_in)
    load_weight = pltpu.make_async_copy(weight_far, weight, weight_in)
    load_grads.start()
    load_weight.start()
    for s in range(S):
        padded[s, 0:line, :] = jnp.zeros((line, CO), BF16)
        padded[s, end:, :] = jnp.zeros((line, CO), BF16)
    load_grads.wait()
    matrix = box[...]
    for s in range(S):
        for R in range(HR):
            window = padded[s, 2 * R * line : (2 * R + 4) * line, :]
            sums = jnp.dot(matrix, window, preferred_element_type=F32).astype(BF16)
            at = (s * HR + R) * W
            for t in range(9):
                g_out[t, at : at + W, :] = sums[t * W : (t + 1) * W]
    load_weight.wait()
    total = jnp.zeros((S * HR * W, C), F32)
    for t in range(9):
        total = total + jnp.dot(g_out[t], weight[t], preferred_element_type=F32)
    acts[...] = total.astype(BF16).reshape(S, HR * W, C)
    me = lax.axis_index("row")
    for d in range(n_row):
        start = pl.multiple_of(lax.rem(me + d, n_row) * (r * W), r * W)
        bands[d][...] = acts[:, pl.ds(start, r * W), :]


def act_kernel(sizes, order, bias, time_weight, feats, prior, *rest):
    S, rW, n_row, F, C = sizes
    outs, (ext, acts) = rest[:n_row], rest[n_row:]
    for f in range(2, F + 2):
        ext[f * rW : (f + 1) * rW, :] = feats[f - 2]
    whole = jnp.where(lax.axis_index("frame") > 0, 1.0, 0.0)
    for f in range(2):
        ext[f * rW : (f + 1) * rW, :] = (prior[F - 2 + f].astype(F32) * whole).astype(BF16)
    row = jnp.concatenate([bias[i : i + 1, :] for i in range(bias.shape[0])], axis=1)
    total = jnp.broadcast_to(row, (F * rW, 2 * C))
    for k in range(3):
        total = total + jnp.dot(
            ext[k * rW : (k + F) * rW, :], time_weight[k], preferred_element_type=F32
        )
    rounded = total.astype(BF16)
    acts[0] = rounded[:, :C].reshape(F, rW, C)
    acts[1] = rounded[:, C:].reshape(F, rW, C)
    me = lax.axis_index("row")
    for d in range(n_row):
        holder = lax.rem(me + d, n_row)
        for s in range(S):
            o = order[holder * S + s]
            outs[d][s] = acts[o % 2, o // 2]


def transposed_acts(sizes, bands, picked):
    S, rW, n_row = sizes
    me = lax.axis_index("row")
    for d in range(n_row):
        source = lax.rem(me - d + n_row, n_row)
        for s in range(S):
            start = pl.multiple_of((s * n_row + source) * rW, rW)
            picked[pl.ds(start, rW), :] = bands[d][s]
    return picked[...].astype(F32).T.astype(BF16)


def all_kernel(sizes, g, *rest):
    n_row, C = sizes[2], rest[0].shape[-1]
    out, picked = rest[n_row:]
    left = transposed_acts(sizes, rest[:n_row], picked)
    for t in range(9):
        out[t * C : (t + 1) * C, :] = jnp.dot(left, g[t], preferred_element_type=F32)


def packed_chunk(plan, index, left, g, terms):
    n_dev, chunk, C, _ = plan
    for value in range(n_dev):

        @pl.when(index == value)
        def _():
            begin, end = value * chunk, (value + 1) * chunk
            for t in range(begin // C, (end + C - 1) // C):
                lo, hi = max(begin, t * C), min(end, (t + 1) * C)
                terms[lo - begin : hi - begin, :] = jnp.dot(
                    left[lo - t * C : hi - t * C, :], g[t], preferred_element_type=F32
                )

    half = chunk // 2
    side = jnp.concatenate([terms[:half, 128:], terms[half:, 128:]], axis=1)
    return jnp.concatenate([terms[:, :128], side], axis=0)


def chunk_index(d, other):
    n_row = lax.axis_size("row")
    frame = lax.axis_index("frame")
    q = jnp.bitwise_xor((frame // 2) * n_row + lax.axis_index("row"), d)
    core = lax.rem(frame, 2)
    return ((q // n_row) * 2 + (1 - core if other else core)) * n_row + lax.rem(q, n_row)


def send_kernel(sizes, plan, group, g, *rest):
    if sizes:
        n_row = sizes[2]
        left, out, picked, terms = rest[n_row:]
        left[...] = transposed_acts(sizes, rest[:n_row], picked)
    else:
        left, out, terms = rest
    for j, d in enumerate(group):
        out[j] = packed_chunk(plan, chunk_index(d, True), left, g, terms).astype(BF16)


def keep_kernel(plan, group, g, left, got, *rest):
    outs, terms = rest[:-1], rest[-1]
    for j, d in enumerate(group):
        value = packed_chunk(plan, chunk_index(d, False), left, g, terms) + got[j].astype(F32)
        outs[j][...] = value.astype(outs[j].dtype)


def square_kernel(scale, keep, *rest):
    value = keep[...]
    for block in rest[:-1]:
        value = value + block[...].astype(F32)
    rest[-1][...] = (value * scale).astype(BF16)


def pair_kernel(mine, got, out):
    out[...] = (mine[...].astype(F32) + got[...].astype(F32)).astype(BF16)


def final_kernel(chunk, CO, mine, got, out, total, even):
    total[...] = mine[...].astype(F32) + got[...].astype(F32)
    half, low = chunk // 2, CO - 128
    side = total[chunk:]
    even[:half, :low] = side[:, :low]
    even[half:, :low] = side[:, low:]
    a, b = (total[pl.ds(p, half, stride=2), :] for p in range(2))
    a_side, b_side = (even[pl.ds(p, half, stride=2), :][:, :low] for p in range(2))
    out[pl.ds(0, half, stride=3), :] = a
    out[pl.ds(1, half, stride=3), :] = jnp.concatenate([a_side, b[:, :low]], axis=1)
    out[pl.ds(2, half, stride=3), :] = jnp.concatenate([b[:, low:], b_side], axis=1)


def order_kernel(sizes, order, *rest):
    S, rW, n_row, _ = sizes
    bands, natural, first = rest[:n_row], rest[n_row], rest[n_row + 1]
    me = lax.axis_index("row")
    for d in range(n_row):
        source = lax.rem(me - d + n_row, n_row)
        for s in range(S):
            o = order[source * S + s]
            start = pl.multiple_of((o // 2) * rW, rW)
            natural[o % 2, pl.ds(start, rW), :] = bands[d][s]
    first[...] = natural[:, : 2 * rW, :]


def input_kernel(sizes, natural, later, time_weight, out, tail):
    rW, F, C = sizes
    tail[:, : F * rW, :] = natural[...]
    n_frame = lax.axis_size("frame")
    whole = jnp.where(lax.axis_index("frame") < n_frame - 1, 1.0, 0.0)
    tail[:, F * rW :, :] = (later[...].astype(F32) * whole).astype(BF16)
    total = jnp.zeros((F * rW, C), F32)
    for k in range(3):
        for p in range(2):
            total = total + lax.dot_general(
                tail[p, (2 - k) * rW : (2 - k + F) * rW, :],
                time_weight[k, :, p * C : (p + 1) * C],
                (((1,), (1,)), ((), ())),
                preferred_element_type=F32,
            )
    out[...] = total.astype(BF16)


def direct(n_frame, n_row, n_clip):
    n_q = n_frame * n_row // 2
    return n_frame % 2 == 0 and 1 < n_q <= 8 and n_q & (n_q - 1) == 0 and n_clip > 1 and n_clip & (n_clip - 1) == 0


def local(features, time_weight, time_bias, space_weight, pixel_grads, frame_order):
    _, F, r, W, C = features.shape
    _, S, UR, UW, CO = pixel_grads.shape
    n_row, n_frame, n_clip = (lax.axis_size(a) for a in ("row", "frame", "clip"))
    HR, rW = r * n_row, r * W
    pixels = S * HR * W
    order = frame_order.reshape(-1)
    both = ("frame", "row")

    feats = features.reshape(F, rW, C)
    forward = [(i, (i + 1) % n_frame) for i in range(n_frame)]
    prior = lax.ppermute(feats, "frame", forward)
    (box,) = kernel_call(
        functools.partial(matrix_kernel, W), [struct((9 * W, 8 * W), BF16)], 0, [], flops=10**10
    )
    g, *bands = kernel_call(
        functools.partial(box_kernel, (S, HR, W, C, CO, r, n_row)),
        [struct((9, pixels, CO), BF16)] + [struct((S, rW, C), BF16)] * n_row,
        0,
        [pixel_grads.reshape(S, UR * UW, CO), space_weight.transpose(0, 1, 3, 2).reshape(9, CO, C), box],
        [
            pltpu.VMEM((S, (UR + 2) * UW, CO), BF16),
            pltpu.VMEM((S, HR * W, C), BF16),
            pltpu.VMEM((9, CO, C), BF16),
            pltpu.SemaphoreType.DMA,
            pltpu.SemaphoreType.DMA,
        ],
        far=(0, 1),
        flops=2 * pixels * 9 * C * CO,
    )

    n_total = 9 * C
    n_dev = n_frame * n_row
    n_q = n_dev // 2
    chunk = n_total // n_dev
    fast = (
        direct(n_frame, n_row, n_clip)
        and n_total % n_dev == 0
        and chunk % 16 == 0
        and CO == 192
    )
    packed = chunk * CO // 128
    own, *others = kernel_call(
        functools.partial(act_kernel, (S, rW, n_row, F, C)),
        [struct((S, rW, C), BF16)] * n_row,
        1,
        [order, time_bias.reshape(-1, 128), time_weight, feats, prior],
        [pltpu.VMEM(((F + 2) * rW, C), BF16), pltpu.VMEM((2, F, rW, C), BF16)],
        flops=2 * F * rW * 6 * C * C,
    )
    acts = [own] + [
        lax.ppermute(others[d - 1], "row", [(i, (i + d) % n_row) for i in range(n_row)])
        for d in range(1, n_row)
    ]
    picked = pltpu.VMEM((pixels, C), BF16)
    flops = 2 * pixels * 9 * C * CO

    scale = 1.0 / math.sqrt(2 * F * UR * UW * n_clip * n_frame)
    if fast:
        plan = (n_dev, chunk, C, CO)
        terms = pltpu.VMEM((chunk, CO), F32)
        groups = [[n_q - 1], list(range(1, n_q - 1)), [0]]
        groups = [group for group in groups if group]
        swap = [(i, ((i // n_row) ^ 1) * n_row + i % n_row) for i in range(n_dev)]

        def square(i, d):
            f, j = i // n_row, i % n_row
            p = ((f // 2) * n_row + j) ^ d
            return ((p // n_row) * 2 + f % 2) * n_row + p % n_row

        got = []
        for k, group in enumerate(groups):
            left_out = [] if k else [struct((C, pixels), BF16)]
            *first, send = kernel_call(
                functools.partial(send_kernel, None if k else (S, rW, n_row), plan, group),
                left_out + [struct((len(group), packed, 128), BF16)],
                0,
                [g] + ([left] if k else acts),
                [terms] if k else [picked, terms],
                flops=flops * len(group) // n_dev,
            )
            left = left if k else first[0]
            swapped = lax.ppermute(send, both, swap)
            shares = kernel_call(
                functools.partial(keep_kernel, plan, group),
                [struct((packed, 128), BF16 if d else F32) for d in group],
                0,
                [g, left, swapped],
                [terms],
                flops=flops * len(group) // n_dev,
            )
            for d, share in zip(group, shares):
                if d:
                    route = [(i, square(i, d)) for i in range(n_dev)]
                    got.append(lax.ppermute(share, both, route))
                else:
                    mine = share
        (mine,) = kernel_call(
            functools.partial(square_kernel, scale), [struct((packed, 128), BF16)], 0, [mine] + got
        )
        mask = n_clip - 1
        while mask:
            got = lax.ppermute(mine, "clip", [(i, i ^ mask) for i in range(n_clip)])
            if mask > 1:
                (mine,) = kernel_call(pair_kernel, [struct((packed, 128), BF16)], 0, [mine, got])
            mask //= 2
        (flat,) = kernel_call(
            functools.partial(final_kernel, chunk, CO),
            [struct((packed, 128), F32)],
            0,
            [mine, got],
            [pltpu.VMEM((packed, 128), F32), pltpu.VMEM((chunk, 128), F32)],
        )
        weight_grad = flat.reshape(-1)
    else:
        (wg,) = kernel_call(
            functools.partial(all_kernel, (S, rW, n_row)),
            [struct((n_total, CO), F32)],
            0,
            [g] + acts,
            [picked],
            flops=flops,
        )
        shard = lax.psum_scatter(wg.reshape(-1), both, scatter_dimension=0, tiled=True)
        weight_grad = lax.psum(shard, "clip") * scale

    bands = [bands[0]] + [
        lax.ppermute(bands[d], "row", [(i, (i + d) % n_row) for i in range(n_row)])
        for d in range(1, n_row)
    ]
    natural, first = kernel_call(
        functools.partial(order_kernel, (S, rW, n_row, F)),
        [struct((2, F * rW, C), BF16), struct((2, 2 * rW, C), BF16)],
        1,
        [order] + bands,
    )
    later = lax.ppermute(first, "frame", [(j, i) for i, j in forward])
    (input_grad,) = kernel_call(
        functools.partial(input_kernel, (rW, F, C)),
        [struct((F * rW, C), BF16)],
        0,
        [natural, later, time_weight],
        [pltpu.VMEM((2, (F + 2) * rW, C), BF16)],
        flops=2 * F * rW * 6 * C * C,
    )
    return input_grad.reshape(features.shape), weight_grad


def solution(mesh):
    step = jax.shard_map(
        local,
        mesh=mesh,
        in_specs=(
            P("clip", "frame", "row", None, None),
            P(),
            P(),
            P(),
            P("clip", ("frame", "row"), None, None, None),
            P("clip", "frame", None),
        ),
        out_specs=(P("clip", "frame", "row", None, None), P(("frame", "row"))),
        check_vma=False,
    )
    if not direct(mesh.shape["frame"], mesh.shape["row"], mesh.shape["clip"]):
        return step
    return step
```

```python
import functools
import math

import jax
import jax.numpy as jnp
from jax import lax
from jax.experimental import pallas as pl
from jax.experimental.pallas import tpu as pltpu
from jax.sharding import PartitionSpec as P


F32 = jnp.float32
BF16 = jnp.bfloat16
VMEM = pl.BlockSpec(memory_space=pltpu.VMEM)
SMEM = pl.BlockSpec(memory_space=pltpu.SMEM)


def struct(shape, dtype):
    return jax.ShapeDtypeStruct(shape, dtype)


def kernel_call(body, outs, n_smem, args, scratch=(), flops=0, far=()):
    moved = sum(math.prod(a.shape) * a.dtype.itemsize for a in list(args) + list(outs))
    specs = [SMEM] * n_smem + [VMEM] * (len(args) - n_smem)
    for i in far:
        specs[i] = pl.BlockSpec(memory_space=pltpu.HBM)
    return pl.pallas_call(
        body,
        out_shape=outs,
        in_specs=specs,
        out_specs=[VMEM] * len(outs),
        scratch_shapes=list(scratch),
        compiler_params=pltpu.CompilerParams(vmem_limit_bytes=16 * 2**20),
        cost_estimate=pl.CostEstimate(flops=flops, bytes_accessed=moved, transcendentals=0),
    )(*args)


def matrix_kernel(width, out):
    column = lax.broadcasted_iota(jnp.int32, (width, 8 * width), 1)
    line, col = column // (2 * width), column % (2 * width)
    first = 2 * lax.broadcasted_iota(jnp.int32, (width, 8 * width), 0) + 1
    for a in range(3):
        rows = (line == 2 - a) | (line == 3 - a)
        for b in range(3):
            inside = rows & ((col == first - b) | (col == first + 1 - b))
            t = 3 * a + b
            out[t * width : (t + 1) * width, :] = jnp.where(inside, 1.0, 0.0).astype(BF16)


def box_kernel(sizes, grads, weight_far, box, g_out, *rest):
    S, HR, W, C, CO, r, n_row = sizes
    bands, (padded, acts, weight, grads_in, weight_in) = rest[:n_row], rest[n_row:]
    line = 2 * W
    end = line * (2 * HR + 1)
    load_grads = pltpu.make_async_copy(grads, padded.at[:, line:end, :], grads_in)
    load_weight = pltpu.make_async_copy(weight_far, weight, weight_in)
    load_grads.start()
    load_weight.start()
    for s in range(S):
        padded[s, 0:line, :] = jnp.zeros((line, CO), BF16)
        padded[s, end:, :] = jnp.zeros((line, CO), BF16)
    load_grads.wait()
    matrix = box[...]
    for s in range(S):
        for R in range(HR):
            window = padded[s, 2 * R * line : (2 * R + 4) * line, :]
            sums = jnp.dot(matrix, window, preferred_element_type=F32).astype(BF16)
            at = (s * HR + R) * W
            for t in range(9):
                g_out[t, at : at + W, :] = sums[t * W : (t + 1) * W]
    load_weight.wait()
    total = jnp.zeros((S * HR * W, C), F32)
    for t in range(9):
        total = total + jnp.dot(g_out[t], weight[t], preferred_element_type=F32)
    acts[...] = total.astype(BF16).reshape(S, HR * W, C)
    me = lax.axis_index("row")
    for d in range(n_row):
        start = pl.multiple_of(lax.rem(me + d, n_row) * (r * W), r * W)
        bands[d][...] = acts[:, pl.ds(start, r * W), :]


def transposed_acts(sizes, order, bias, time_weight, bands, ext, acts, picked):
    S, rW, n_row, F, C = sizes
    step = n_row * rW
    own, prior = bands[:n_row], bands[n_row:]
    me = lax.axis_index("row")
    whole = jnp.where(lax.axis_index("frame") > 0, 1.0, 0.0)
    for d in range(n_row):
        source = lax.rem(me - d + n_row, n_row)
        for f in range(F + 2):
            start = pl.multiple_of(f * step + source * rW, rW)
            if f < 2:
                block = (prior[d][F - 2 + f].astype(F32) * whole).astype(BF16)
            else:
                block = own[d][f - 2]
            ext[pl.ds(start, rW), :] = block
    row = jnp.concatenate([bias[i : i + 1, :] for i in range(bias.shape[0])], axis=1)
    total = jnp.broadcast_to(row, (F * step, 2 * C))
    for k in range(3):
        total = total + jnp.dot(
            ext[k * step : (k + F) * step, :], time_weight[k], preferred_element_type=F32
        )
    rounded = total.astype(BF16)
    acts[0] = rounded[:, :C]
    acts[1] = rounded[:, C:]
    for s in range(S):
        o = order[me * S + s]
        start = pl.multiple_of((o // 2) * step, step)
        picked[s * step : (s + 1) * step, :] = acts[o % 2, pl.ds(start, step), :]
    return picked[...].astype(F32).T.astype(BF16)


def all_kernel(sizes, order, bias, time_weight, g, *rest):
    n_row, C = sizes[2], sizes[4]
    out, *scratch = rest[2 * n_row :]
    left = transposed_acts(sizes, order, bias, time_weight, rest[: 2 * n_row], *scratch)
    for t in range(9):
        out[t * C : (t + 1) * C, :] = jnp.dot(left, g[t], preferred_element_type=F32)


def packed_chunk(plan, index, left, g, terms):
    n_dev, chunk, C, _ = plan
    for value in range(n_dev):

        @pl.when(index == value)
        def _():
            begin, end = value * chunk, (value + 1) * chunk
            for t in range(begin // C, (end + C - 1) // C):
                lo, hi = max(begin, t * C), min(end, (t + 1) * C)
                terms[lo - begin : hi - begin, :] = jnp.dot(
                    left[lo - t * C : hi - t * C, :], g[t], preferred_element_type=F32
                )

    half = chunk // 2
    side = jnp.concatenate([terms[:half, 128:], terms[half:, 128:]], axis=1)
    return jnp.concatenate([terms[:, :128], side], axis=0)


def chunk_index(d, other):
    n_row = lax.axis_size("row")
    frame = lax.axis_index("frame")
    q = jnp.bitwise_xor((frame // 2) * n_row + lax.axis_index("row"), d)
    core = lax.rem(frame, 2)
    return ((q // n_row) * 2 + (1 - core if other else core)) * n_row + lax.rem(q, n_row)


def send_kernel(sizes, plan, group, *rest):
    if sizes:
        order, bias, time_weight, g, *rest = rest
        n_row = sizes[2]
        left, out, *scratch, terms = rest[2 * n_row :]
        left[...] = transposed_acts(sizes, order, bias, time_weight, rest[: 2 * n_row], *scratch)
    else:
        g, left, out, terms = rest
    for j, d in enumerate(group):
        out[j] = packed_chunk(plan, chunk_index(d, True), left, g, terms).astype(BF16)


def keep_kernel(plan, group, g, left, got, *rest):
    outs, terms = rest[:-1], rest[-1]
    for j, d in enumerate(group):
        value = packed_chunk(plan, chunk_index(d, False), left, g, terms) + got[j].astype(F32)
        outs[j][...] = value.astype(outs[j].dtype)


def square_kernel(scale, keep, *rest):
    value = keep[...]
    for block in rest[:-1]:
        value = value + block[...].astype(F32)
    rest[-1][...] = (value * scale).astype(BF16)


def pair_kernel(mine, got, out):
    out[...] = (mine[...].astype(F32) + got[...].astype(F32)).astype(BF16)


def final_kernel(chunk, CO, mine, got, out, total, even):
    total[...] = mine[...].astype(F32) + got[...].astype(F32)
    half, low = chunk // 2, CO - 128
    side = total[chunk:]
    even[:half, :low] = side[:, :low]
    even[half:, :low] = side[:, low:]
    a, b = (total[pl.ds(p, half, stride=2), :] for p in range(2))
    a_side, b_side = (even[pl.ds(p, half, stride=2), :][:, :low] for p in range(2))
    out[pl.ds(0, half, stride=3), :] = a
    out[pl.ds(1, half, stride=3), :] = jnp.concatenate([a_side, b[:, :low]], axis=1)
    out[pl.ds(2, half, stride=3), :] = jnp.concatenate([b[:, low:], b_side], axis=1)


def order_kernel(sizes, order, *rest):
    S, rW, n_row, _ = sizes
    bands, natural, first = rest[:n_row], rest[n_row], rest[n_row + 1]
    me = lax.axis_index("row")
    for d in range(n_row):
        source = lax.rem(me - d + n_row, n_row)
        for s in range(S):
            o = order[source * S + s]
            start = pl.multiple_of((o // 2) * rW, rW)
            natural[o % 2, pl.ds(start, rW), :] = bands[d][s]
    first[...] = natural[:, : 2 * rW, :]


def input_kernel(sizes, natural, later, time_weight, out, tail):
    rW, F, C = sizes
    tail[:, : F * rW, :] = natural[...]
    n_frame = lax.axis_size("frame")
    whole = jnp.where(lax.axis_index("frame") < n_frame - 1, 1.0, 0.0)
    tail[:, F * rW :, :] = (later[...].astype(F32) * whole).astype(BF16)
    total = jnp.zeros((F * rW, C), F32)
    for k in range(3):
        for p in range(2):
            total = total + lax.dot_general(
                tail[p, (2 - k) * rW : (2 - k + F) * rW, :],
                time_weight[k, :, p * C : (p + 1) * C],
                (((1,), (1,)), ((), ())),
                preferred_element_type=F32,
            )
    out[...] = total.astype(BF16)


def direct(n_frame, n_row, n_clip):
    n_q = n_frame * n_row // 2
    return n_frame % 2 == 0 and 1 < n_q <= 8 and n_q & (n_q - 1) == 0 and n_clip > 1 and n_clip & (n_clip - 1) == 0


def local(features, time_weight, time_bias, space_weight, pixel_grads, frame_order):
    _, F, r, W, C = features.shape
    _, S, UR, UW, CO = pixel_grads.shape
    n_row, n_frame, n_clip = (lax.axis_size(a) for a in ("row", "frame", "clip"))
    HR, rW = r * n_row, r * W
    pixels = S * HR * W
    order = frame_order.reshape(-1)
    both = ("frame", "row")

    feats = features.reshape(F, rW, C)
    forward = [(i, (i + 1) % n_frame) for i in range(n_frame)]
    prior = [lax.ppermute(feats, "frame", forward)]
    own = [feats] + [
        lax.ppermute(feats, "row", [(i, (i + d) % n_row) for i in range(n_row)])
        for d in range(1, n_row)
    ]
    for d in range(1, n_row):
        route = [(i * n_row + k, j * n_row + (k + d) % n_row) for i, j in forward for k in range(n_row)]
        prior.append(lax.ppermute(feats, both, route))
    (box,) = kernel_call(
        functools.partial(matrix_kernel, W), [struct((9 * W, 8 * W), BF16)], 0, [], flops=10**10
    )
    g, *bands = kernel_call(
        functools.partial(box_kernel, (S, HR, W, C, CO, r, n_row)),
        [struct((9, pixels, CO), BF16)] + [struct((S, rW, C), BF16)] * n_row,
        0,
        [pixel_grads.reshape(S, UR * UW, CO), space_weight.transpose(0, 1, 3, 2).reshape(9, CO, C), box],
        [
            pltpu.VMEM((S, (UR + 2) * UW, CO), BF16),
            pltpu.VMEM((S, HR * W, C), BF16),
            pltpu.VMEM((9, CO, C), BF16),
            pltpu.SemaphoreType.DMA,
            pltpu.SemaphoreType.DMA,
        ],
        far=(0, 1),
        flops=2 * pixels * 9 * C * CO,
    )

    n_total = 9 * C
    n_dev = n_frame * n_row
    n_q = n_dev // 2
    chunk = n_total // n_dev
    fast = (
        direct(n_frame, n_row, n_clip)
        and n_total % n_dev == 0
        and chunk % 16 == 0
        and CO == 192
    )
    packed = chunk * CO // 128
    inputs = [order, time_bias.reshape(-1, 128), time_weight, g] + own + prior
    ext = [
        pltpu.VMEM(((F + 2) * HR * W, C), BF16),
        pltpu.VMEM((2, F * HR * W, C), BF16),
        pltpu.VMEM((pixels, C), BF16),
    ]
    sizes = (S, rW, n_row, F, C)
    flops = 2 * pixels * 9 * C * CO

    scale = 1.0 / math.sqrt(2 * F * UR * UW * n_clip * n_frame)
    if fast:
        plan = (n_dev, chunk, C, CO)
        terms = pltpu.VMEM((chunk, CO), F32)
        groups = [[n_q - 1], list(range(1, n_q - 1)), [0]]
        groups = [group for group in groups if group]
        swap = [(i, ((i // n_row) ^ 1) * n_row + i % n_row) for i in range(n_dev)]

        def square(i, d):
            f, j = i // n_row, i % n_row
            p = ((f // 2) * n_row + j) ^ d
            return ((p // n_row) * 2 + f % 2) * n_row + p % n_row

        got = []
        for k, group in enumerate(groups):
            left_out = [] if k else [struct((C, pixels), BF16)]
            *first, send = kernel_call(
                functools.partial(send_kernel, None if k else sizes, plan, group),
                left_out + [struct((len(group), packed, 128), BF16)],
                0 if k else 1,
                [g, left] if k else inputs,
                [terms] if k else ext + [terms],
                flops=flops * len(group) // n_dev,
            )
            left = left if k else first[0]
            swapped = lax.ppermute(send, both, swap)
            shares = kernel_call(
                functools.partial(keep_kernel, plan, group),
                [struct((packed, 128), BF16 if d else F32) for d in group],
                0,
                [g, left, swapped],
                [terms],
                flops=flops * len(group) // n_dev,
            )
            for d, share in zip(group, shares):
                if d:
                    route = [(i, square(i, d)) for i in range(n_dev)]
                    got.append(lax.ppermute(share, both, route))
                else:
                    mine = share
        (mine,) = kernel_call(
            functools.partial(square_kernel, scale), [struct((packed, 128), BF16)], 0, [mine] + got
        )
        mask = n_clip - 1
        while mask:
            got = lax.ppermute(mine, "clip", [(i, i ^ mask) for i in range(n_clip)])
            if mask > 1:
                (mine,) = kernel_call(pair_kernel, [struct((packed, 128), BF16)], 0, [mine, got])
            mask //= 2
        (flat,) = kernel_call(
            functools.partial(final_kernel, chunk, CO),
            [struct((packed, 128), F32)],
            0,
            [mine, got],
            [pltpu.VMEM((packed, 128), F32), pltpu.VMEM((chunk, 128), F32)],
        )
        weight_grad = flat.reshape(-1)
    else:
        (wg,) = kernel_call(
            functools.partial(all_kernel, sizes),
            [struct((n_total, CO), F32)],
            1,
            inputs,
            ext,
            flops=flops,
        )
        shard = lax.psum_scatter(wg.reshape(-1), both, scatter_dimension=0, tiled=True)
        weight_grad = lax.psum(shard, "clip") * scale

    bands = [bands[0]] + [
        lax.ppermute(bands[d], "row", [(i, (i + d) % n_row) for i in range(n_row)])
        for d in range(1, n_row)
    ]
    natural, first = kernel_call(
        functools.partial(order_kernel, (S, rW, n_row, F)),
        [struct((2, F * rW, C), BF16), struct((2, 2 * rW, C), BF16)],
        1,
        [order] + bands,
    )
    later = lax.ppermute(first, "frame", [(j, i) for i, j in forward])
    (input_grad,) = kernel_call(
        functools.partial(input_kernel, (rW, F, C)),
        [struct((F * rW, C), BF16)],
        0,
        [natural, later, time_weight],
        [pltpu.VMEM((2, (F + 2) * rW, C), BF16)],
        flops=2 * F * rW * 6 * C * C,
    )
    return input_grad.reshape(features.shape), weight_grad


def solution(mesh):
    step = jax.shard_map(
        local,
        mesh=mesh,
        in_specs=(
            P("clip", "frame", "row", None, None),
            P(),
            P(),
            P(),
            P("clip", ("frame", "row"), None, None, None),
            P("clip", "frame", None),
        ),
        out_specs=(P("clip", "frame", "row", None, None), P(("frame", "row"))),
        check_vma=False,
    )
    if not direct(mesh.shape["frame"], mesh.shape["row"], mesh.shape["clip"]):
        return step
    return step
```

```python
import functools
import math

import jax
import jax.numpy as jnp
from jax import lax
from jax.experimental import pallas as pl
from jax.experimental.pallas import tpu as pltpu
from jax.sharding import PartitionSpec as P


F32 = jnp.float32
BF16 = jnp.bfloat16
VMEM = pl.BlockSpec(memory_space=pltpu.VMEM)
SMEM = pl.BlockSpec(memory_space=pltpu.SMEM)


def struct(shape, dtype):
    return jax.ShapeDtypeStruct(shape, dtype)


def kernel_call(body, outs, n_smem, args, scratch=(), flops=0, far=()):
    moved = sum(math.prod(a.shape) * a.dtype.itemsize for a in list(args) + list(outs))
    specs = [SMEM] * n_smem + [VMEM] * (len(args) - n_smem)
    for i in far:
        specs[i] = pl.BlockSpec(memory_space=pltpu.HBM)
    return pl.pallas_call(
        body,
        out_shape=outs,
        in_specs=specs,
        out_specs=[VMEM] * len(outs),
        scratch_shapes=list(scratch),
        compiler_params=pltpu.CompilerParams(vmem_limit_bytes=16 * 2**20),
        cost_estimate=pl.CostEstimate(flops=flops, bytes_accessed=moved, transcendentals=0),
    )(*args)


def matrix_kernel(width, out):
    column = lax.broadcasted_iota(jnp.int32, (width, 8 * width), 1)
    line, col = column // (2 * width), column % (2 * width)
    first = 2 * lax.broadcasted_iota(jnp.int32, (width, 8 * width), 0) + 1
    for a in range(3):
        rows = (line == 2 - a) | (line == 3 - a)
        for b in range(3):
            inside = rows & ((col == first - b) | (col == first + 1 - b))
            t = 3 * a + b
            out[t * width : (t + 1) * width, :] = jnp.where(inside, 1.0, 0.0).astype(BF16)


def box_kernel(sizes, grads, weight_far, box, g_out, *rest):
    S, HR, W, C, CO, r, n_row = sizes
    bands, (padded, acts, weight, grads_in, weight_in) = rest[:n_row], rest[n_row:]
    line = 2 * W
    end = line * (2 * HR + 1)
    load_grads = pltpu.make_async_copy(grads, padded.at[:, line:end, :], grads_in)
    load_weight = pltpu.make_async_copy(weight_far, weight, weight_in)
    load_grads.start()
    load_weight.start()
    for s in range(S):
        padded[s, 0:line, :] = jnp.zeros((line, CO), BF16)
        padded[s, end:, :] = jnp.zeros((line, CO), BF16)
    load_grads.wait()
    matrix = box[...]
    for s in range(S):
        for R in range(HR):
            window = padded[s, 2 * R * line : (2 * R + 4) * line, :]
            sums = jnp.dot(matrix, window, preferred_element_type=F32).astype(BF16)
            at = (s * HR + R) * W
            for t in range(9):
                g_out[t, at : at + W, :] = sums[t * W : (t + 1) * W]
    load_weight.wait()
    total = jnp.zeros((S * HR * W, C), F32)
    for t in range(9):
        total = total + jnp.dot(g_out[t], weight[t], preferred_element_type=F32)
    acts[...] = total.astype(BF16).reshape(S, HR * W, C)
    me = lax.axis_index("row")
    for d in range(n_row):
        start = pl.multiple_of(lax.rem(me + d, n_row) * (r * W), r * W)
        bands[d][...] = acts[:, pl.ds(start, r * W), :]


def transposed_acts(sizes, order, bias, time_weight, bands, ext, acts, picked):
    S, rW, n_row, F, C = sizes
    step = n_row * rW
    own, prior = bands[:n_row], bands[n_row:]
    me = lax.axis_index("row")
    whole = jnp.where(lax.axis_index("frame") > 0, 1.0, 0.0)
    for d in range(n_row):
        source = lax.rem(me - d + n_row, n_row)
        for f in range(F + 2):
            start = pl.multiple_of(f * step + source * rW, rW)
            if f < 2:
                block = (prior[d][F - 2 + f].astype(F32) * whole).astype(BF16)
            else:
                block = own[d][f - 2]
            ext[pl.ds(start, rW), :] = block
    row = jnp.concatenate([bias[i : i + 1, :] for i in range(bias.shape[0])], axis=1)
    total = jnp.broadcast_to(row, (F * step, 2 * C))
    for k in range(3):
        total = total + jnp.dot(
            ext[k * step : (k + F) * step, :], time_weight[k], preferred_element_type=F32
        )
    rounded = total.astype(BF16)
    acts[0] = rounded[:, :C]
    acts[1] = rounded[:, C:]
    for s in range(S):
        o = order[me * S + s]
        start = pl.multiple_of((o // 2) * step, step)
        picked[s * step : (s + 1) * step, :] = acts[o % 2, pl.ds(start, step), :]
    return picked[...].astype(F32).T.astype(BF16)


def all_kernel(sizes, order, bias, time_weight, g, *rest):
    n_row, C = sizes[2], sizes[4]
    out, *scratch = rest[2 * n_row :]
    left = transposed_acts(sizes, order, bias, time_weight, rest[: 2 * n_row], *scratch)
    for t in range(9):
        out[t * C : (t + 1) * C, :] = jnp.dot(left, g[t], preferred_element_type=F32)


def packed_chunk(plan, index, left, g, terms):
    n_dev, chunk, C, _ = plan
    for value in range(n_dev):

        @pl.when(index == value)
        def _():
            begin, end = value * chunk, (value + 1) * chunk
            for t in range(begin // C, (end + C - 1) // C):
                lo, hi = max(begin, t * C), min(end, (t + 1) * C)
                terms[lo - begin : hi - begin, :] = jnp.dot(
                    left[lo - t * C : hi - t * C, :], g[t], preferred_element_type=F32
                )

    half = chunk // 2
    side = jnp.concatenate([terms[:half, 128:], terms[half:, 128:]], axis=1)
    return jnp.concatenate([terms[:, :128], side], axis=0)


def chunk_index(d, other):
    n_row = lax.axis_size("row")
    frame = lax.axis_index("frame")
    q = jnp.bitwise_xor((frame // 2) * n_row + lax.axis_index("row"), d)
    core = lax.rem(frame, 2)
    return ((q // n_row) * 2 + (1 - core if other else core)) * n_row + lax.rem(q, n_row)


def send_kernel(sizes, plan, group, *rest):
    if sizes:
        order, bias, time_weight, g, *rest = rest
        n_row = sizes[2]
        left, out, *scratch, terms = rest[2 * n_row :]
        left[...] = transposed_acts(sizes, order, bias, time_weight, rest[: 2 * n_row], *scratch)
    else:
        g, left, out, terms = rest
    for j, d in enumerate(group):
        out[j] = packed_chunk(plan, chunk_index(d, True), left, g, terms).astype(BF16)


def keep_kernel(plan, group, g, left, got, *rest):
    outs, terms = rest[:-1], rest[-1]
    for j, d in enumerate(group):
        value = packed_chunk(plan, chunk_index(d, False), left, g, terms) + got[j].astype(F32)
        outs[j][...] = value.astype(outs[j].dtype)


def square_kernel(scale, keep, *rest):
    value = keep[...]
    for block in rest[:-1]:
        value = value + block[...].astype(F32)
    rest[-1][...] = (value * scale).astype(BF16)


def pair_kernel(mine, got, out):
    out[...] = (mine[...].astype(F32) + got[...].astype(F32)).astype(BF16)


def final_kernel(chunk, CO, mine, got, out, total, even):
    total[...] = mine[...].astype(F32) + got[...].astype(F32)
    half, low = chunk // 2, CO - 128
    side = total[chunk:]
    even[:half, :low] = side[:, :low]
    even[half:, :low] = side[:, low:]
    a, b = (total[pl.ds(p, half, stride=2), :] for p in range(2))
    a_side, b_side = (even[pl.ds(p, half, stride=2), :][:, :low] for p in range(2))
    out[pl.ds(0, half, stride=3), :] = a
    out[pl.ds(1, half, stride=3), :] = jnp.concatenate([a_side, b[:, :low]], axis=1)
    out[pl.ds(2, half, stride=3), :] = jnp.concatenate([b[:, low:], b_side], axis=1)


def order_kernel(sizes, order, *rest):
    S, rW, n_row, _ = sizes
    bands, natural, first = rest[:n_row], rest[n_row], rest[n_row + 1]
    me = lax.axis_index("row")
    for d in range(n_row):
        source = lax.rem(me - d + n_row, n_row)
        for s in range(S):
            o = order[source * S + s]
            start = pl.multiple_of((o // 2) * rW, rW)
            natural[o % 2, pl.ds(start, rW), :] = bands[d][s]
    first[...] = natural[:, : 2 * rW, :]


def input_kernel(sizes, natural, later, time_weight, out, tail):
    rW, F, C = sizes
    tail[:, : F * rW, :] = natural[...]
    n_frame = lax.axis_size("frame")
    whole = jnp.where(lax.axis_index("frame") < n_frame - 1, 1.0, 0.0)
    tail[:, F * rW :, :] = (later[...].astype(F32) * whole).astype(BF16)
    total = jnp.zeros((F * rW, C), F32)
    for k in range(3):
        for p in range(2):
            total = total + lax.dot_general(
                tail[p, (2 - k) * rW : (2 - k + F) * rW, :],
                time_weight[k, :, p * C : (p + 1) * C],
                (((1,), (1,)), ((), ())),
                preferred_element_type=F32,
            )
    out[...] = total.astype(BF16)


def direct(n_frame, n_row, n_clip):
    n_q = n_frame * n_row // 2
    return n_frame % 2 == 0 and 1 < n_q <= 8 and n_q & (n_q - 1) == 0 and n_clip > 1 and n_clip & (n_clip - 1) == 0


def local(features, time_weight, time_bias, space_weight, pixel_grads, frame_order):
    _, F, r, W, C = features.shape
    _, S, UR, UW, CO = pixel_grads.shape
    n_row, n_frame, n_clip = (lax.axis_size(a) for a in ("row", "frame", "clip"))
    HR, rW = r * n_row, r * W
    pixels = S * HR * W
    order = frame_order.reshape(-1)
    both = ("frame", "row")

    feats = features.reshape(F, rW, C)
    forward = [(i, (i + 1) % n_frame) for i in range(n_frame)]
    prior = [lax.ppermute(feats, "frame", forward)]
    own = [feats] + [
        lax.ppermute(feats, "row", [(i, (i + d) % n_row) for i in range(n_row)])
        for d in range(1, n_row)
    ]
    for d in range(1, n_row):
        route = [(i * n_row + k, j * n_row + (k + d) % n_row) for i, j in forward for k in range(n_row)]
        prior.append(lax.ppermute(feats, both, route))
    (box,) = kernel_call(
        functools.partial(matrix_kernel, W), [struct((9 * W, 8 * W), BF16)], 0, [], flops=10**10
    )
    g, *bands = kernel_call(
        functools.partial(box_kernel, (S, HR, W, C, CO, r, n_row)),
        [struct((9, pixels, CO), BF16)] + [struct((S, rW, C), BF16)] * n_row,
        0,
        [pixel_grads.reshape(S, UR * UW, CO), space_weight.transpose(0, 1, 3, 2).reshape(9, CO, C), box],
        [
            pltpu.VMEM((S, (UR + 2) * UW, CO), BF16),
            pltpu.VMEM((S, HR * W, C), BF16),
            pltpu.VMEM((9, CO, C), BF16),
            pltpu.SemaphoreType.DMA,
            pltpu.SemaphoreType.DMA,
        ],
        far=(0, 1),
        flops=2 * pixels * 9 * C * CO,
    )

    n_total = 9 * C
    n_dev = n_frame * n_row
    n_q = n_dev // 2
    chunk = n_total // n_dev
    fast = (
        direct(n_frame, n_row, n_clip)
        and n_total % n_dev == 0
        and chunk % 16 == 0
        and CO == 192
    )
    packed = chunk * CO // 128
    inputs = [order, time_bias.reshape(-1, 128), time_weight, g] + own + prior
    ext = [
        pltpu.VMEM(((F + 2) * HR * W, C), BF16),
        pltpu.VMEM((2, F * HR * W, C), BF16),
        pltpu.VMEM((pixels, C), BF16),
    ]
    sizes = (S, rW, n_row, F, C)
    flops = 2 * pixels * 9 * C * CO

    scale = 1.0 / math.sqrt(2 * F * UR * UW * n_clip * n_frame)
    if fast:
        plan = (n_dev, chunk, C, CO)
        terms = pltpu.VMEM((chunk, CO), F32)
        groups = [[n_q - 1], list(range(1, n_q - 1)), [0]]
        groups = [group for group in groups if group]
        swap = [(i, ((i // n_row) ^ 1) * n_row + i % n_row) for i in range(n_dev)]

        def square(i, d):
            f, j = i // n_row, i % n_row
            p = ((f // 2) * n_row + j) ^ d
            return ((p // n_row) * 2 + f % 2) * n_row + p % n_row

        got = []
        for k, group in enumerate(groups):
            left_out = [] if k else [struct((C, pixels), BF16)]
            *first, send = kernel_call(
                functools.partial(send_kernel, None if k else sizes, plan, group),
                left_out + [struct((len(group), packed, 128), BF16)],
                0 if k else 1,
                [g, left] if k else inputs,
                [terms] if k else ext + [terms],
                flops=flops * len(group) // n_dev,
            )
            left = left if k else first[0]
            swapped = lax.ppermute(send, both, swap)
            shares = kernel_call(
                functools.partial(keep_kernel, plan, group),
                [struct((packed, 128), BF16 if d else F32) for d in group],
                0,
                [g, left, swapped],
                [terms],
                flops=flops * len(group) // n_dev,
            )
            for d, share in zip(group, shares):
                if d:
                    route = [(i, square(i, d)) for i in range(n_dev)]
                    got.append(lax.ppermute(share, both, route))
                else:
                    mine = share
        (mine,) = kernel_call(
            functools.partial(square_kernel, scale), [struct((packed, 128), BF16)], 0, [mine] + got
        )
        masks = [(1 << k) - 1 for k in range(1, n_clip.bit_length())]
        for mask in masks:
            got = lax.ppermute(mine, "clip", [(i, i ^ mask) for i in range(n_clip)])
            if mask != masks[-1]:
                (mine,) = kernel_call(pair_kernel, [struct((packed, 128), BF16)], 0, [mine, got])
        (flat,) = kernel_call(
            functools.partial(final_kernel, chunk, CO),
            [struct((packed, 128), F32)],
            0,
            [mine, got],
            [pltpu.VMEM((packed, 128), F32), pltpu.VMEM((chunk, 128), F32)],
        )
        weight_grad = flat.reshape(-1)
    else:
        (wg,) = kernel_call(
            functools.partial(all_kernel, sizes),
            [struct((n_total, CO), F32)],
            1,
            inputs,
            ext,
            flops=flops,
        )
        shard = lax.psum_scatter(wg.reshape(-1), both, scatter_dimension=0, tiled=True)
        weight_grad = lax.psum(shard, "clip") * scale

    bands = [bands[0]] + [
        lax.ppermute(bands[d], "row", [(i, (i + d) % n_row) for i in range(n_row)])
        for d in range(1, n_row)
    ]
    natural, first = kernel_call(
        functools.partial(order_kernel, (S, rW, n_row, F)),
        [struct((2, F * rW, C), BF16), struct((2, 2 * rW, C), BF16)],
        1,
        [order] + bands,
    )
    later = lax.ppermute(first, "frame", [(j, i) for i, j in forward])
    (input_grad,) = kernel_call(
        functools.partial(input_kernel, (rW, F, C)),
        [struct((F * rW, C), BF16)],
        0,
        [natural, later, time_weight],
        [pltpu.VMEM((2, (F + 2) * rW, C), BF16)],
        flops=2 * F * rW * 6 * C * C,
    )
    return input_grad.reshape(features.shape), weight_grad


def solution(mesh):
    step = jax.shard_map(
        local,
        mesh=mesh,
        in_specs=(
            P("clip", "frame", "row", None, None),
            P(),
            P(),
            P(),
            P("clip", ("frame", "row"), None, None, None),
            P("clip", "frame", None),
        ),
        out_specs=(P("clip", "frame", "row", None, None), P(("frame", "row"))),
        check_vma=False,
    )
    if not direct(mesh.shape["frame"], mesh.shape["row"], mesh.shape["clip"]):
        return step
    return step
```

```python
import functools
import math

import jax
import jax.numpy as jnp
from jax import lax
from jax.experimental import pallas as pl
from jax.experimental.pallas import tpu as pltpu
from jax.sharding import PartitionSpec as P


F32 = jnp.float32
BF16 = jnp.bfloat16
VMEM = pl.BlockSpec(memory_space=pltpu.VMEM)
SMEM = pl.BlockSpec(memory_space=pltpu.SMEM)


def struct(shape, dtype):
    return jax.ShapeDtypeStruct(shape, dtype)


def kernel_call(body, outs, n_smem, args, scratch=(), flops=0, far=()):
    moved = sum(math.prod(a.shape) * a.dtype.itemsize for a in list(args) + list(outs))
    specs = [SMEM] * n_smem + [VMEM] * (len(args) - n_smem)
    for i in far:
        specs[i] = pl.BlockSpec(memory_space=pltpu.HBM)
    return pl.pallas_call(
        body,
        out_shape=outs,
        in_specs=specs,
        out_specs=[VMEM] * len(outs),
        scratch_shapes=list(scratch),
        compiler_params=pltpu.CompilerParams(vmem_limit_bytes=16 * 2**20),
        cost_estimate=pl.CostEstimate(flops=flops, bytes_accessed=moved, transcendentals=0),
    )(*args)


def matrix_kernel(width, out):
    column = lax.broadcasted_iota(jnp.int32, (width, 8 * width), 1)
    line, col = column // (2 * width), column % (2 * width)
    first = 2 * lax.broadcasted_iota(jnp.int32, (width, 8 * width), 0) + 1
    for a in range(3):
        rows = (line == 2 - a) | (line == 3 - a)
        for b in range(3):
            inside = rows & ((col == first - b) | (col == first + 1 - b))
            t = 3 * a + b
            out[t * width : (t + 1) * width, :] = jnp.where(inside, 1.0, 0.0).astype(BF16)


def box_kernel(sizes, grads, weight_far, box, g_out, *rest):
    S, HR, W, C, CO, r, n_row = sizes
    bands, (padded, acts, weight, grads_in, weight_in) = rest[:n_row], rest[n_row:]
    line = 2 * W
    end = line * (2 * HR + 1)
    load_grads = pltpu.make_async_copy(grads, padded.at[:, line:end, :], grads_in)
    load_weight = pltpu.make_async_copy(weight_far, weight, weight_in)
    load_grads.start()
    load_weight.start()
    for s in range(S):
        padded[s, 0:line, :] = jnp.zeros((line, CO), BF16)
        padded[s, end:, :] = jnp.zeros((line, CO), BF16)
    load_grads.wait()
    matrix = box[...]
    for s in range(S):
        for R in range(HR):
            window = padded[s, 2 * R * line : (2 * R + 4) * line, :]
            sums = jnp.dot(matrix, window, preferred_element_type=F32).astype(BF16)
            at = (s * HR + R) * W
            for t in range(9):
                g_out[t, at : at + W, :] = sums[t * W : (t + 1) * W]
    load_weight.wait()
    total = jnp.zeros((S * HR * W, C), F32)
    for t in range(9):
        total = total + jnp.dot(g_out[t], weight[t], preferred_element_type=F32)
    acts[...] = total.astype(BF16).reshape(S, HR * W, C)
    me = lax.axis_index("row")
    for d in range(n_row):
        start = pl.multiple_of(lax.rem(me + d, n_row) * (r * W), r * W)
        bands[d][...] = acts[:, pl.ds(start, r * W), :]


def extended(sizes, ext, bands):
    rW, n_row = sizes[1], sizes[2]
    me = lax.axis_index("row")
    for d in range(n_row):
        source = lax.rem(me - d + n_row, n_row)
        for f, block in enumerate(bands(d)):
            start = pl.multiple_of(f * n_row * rW + source * rW, rW)
            ext[pl.ds(start, rW), :] = block


def time_conv(sizes, frames, bias, time_weight, ext, acts):
    _, rW, n_row, _, C = sizes
    step = n_row * rW
    row = jnp.concatenate([bias[i : i + 1, :] for i in range(bias.shape[0])], axis=1)
    total = jnp.broadcast_to(row, (frames * step, 2 * C))
    for k in range(3):
        total = total + jnp.dot(
            ext[k * step : (k + frames) * step, :], time_weight[k], preferred_element_type=F32
        )
    rounded = total.astype(BF16).reshape(frames, step, 2 * C)
    acts[0] = rounded[:, :, :C]
    acts[1] = rounded[:, :, C:]


def late_kernel(sizes, bias, time_weight, *rest):
    n_row, F = sizes[2], sizes[3]
    own, (acts, ext) = rest[:n_row], rest[n_row:]
    extended(sizes, ext, lambda d: [own[d][f] for f in range(F)])
    time_conv(sizes, F - 2, bias, time_weight, ext, acts)


def transposed_acts(sizes, order, bias, time_weight, late, bands, ext, early, picked):
    S, rW, n_row, F, _ = sizes
    step = n_row * rW
    own, prior = bands[:n_row], bands[n_row:]
    whole = jnp.where(lax.axis_index("frame") > 0, 1.0, 0.0)

    def frames(d):
        before = [(prior[d][f].astype(F32) * whole).astype(BF16) for f in range(F - 2, F)]
        return before + [own[d][f] for f in range(2)]

    extended(sizes, ext, frames)
    time_conv(sizes, 2, bias, time_weight, ext, early)
    me = lax.axis_index("row")
    for s in range(S):
        o = order[me * S + s]
        f = o // 2

        @pl.when(f < 2)
        def _():
            picked[s * step : (s + 1) * step, :] = early[o % 2, f]

        @pl.when(f >= 2)
        def _():
            picked[s * step : (s + 1) * step, :] = late[o % 2, f - 2]

    return picked[...].astype(F32).T.astype(BF16)


def all_kernel(sizes, order, bias, time_weight, late, g, *rest):
    n_row, C = sizes[2], sizes[4]
    out, *scratch = rest[2 * n_row :]
    left = transposed_acts(sizes, order, bias, time_weight, late, rest[: 2 * n_row], *scratch)
    for t in range(9):
        out[t * C : (t + 1) * C, :] = jnp.dot(left, g[t], preferred_element_type=F32)


def packed_chunk(plan, index, left, g, terms):
    n_dev, chunk, C, _ = plan
    for value in range(n_dev):

        @pl.when(index == value)
        def _():
            begin, end = value * chunk, (value + 1) * chunk
            for t in range(begin // C, (end + C - 1) // C):
                lo, hi = max(begin, t * C), min(end, (t + 1) * C)
                terms[lo - begin : hi - begin, :] = jnp.dot(
                    left[lo - t * C : hi - t * C, :], g[t], preferred_element_type=F32
                )

    half = chunk // 2
    side = jnp.concatenate([terms[:half, 128:], terms[half:, 128:]], axis=1)
    return jnp.concatenate([terms[:, :128], side], axis=0)


def chunk_index(d, other):
    n_row = lax.axis_size("row")
    frame = lax.axis_index("frame")
    q = jnp.bitwise_xor((frame // 2) * n_row + lax.axis_index("row"), d)
    core = lax.rem(frame, 2)
    return ((q // n_row) * 2 + (1 - core if other else core)) * n_row + lax.rem(q, n_row)


def send_kernel(sizes, plan, group, *rest):
    if sizes:
        order, bias, time_weight, late, g, *rest = rest
        n_row = sizes[2]
        left, out, *scratch, terms = rest[2 * n_row :]
        left[...] = transposed_acts(sizes, order, bias, time_weight, late, rest[: 2 * n_row], *scratch)
    else:
        g, left, out, terms = rest
    for j, d in enumerate(group):
        out[j] = packed_chunk(plan, chunk_index(d, True), left, g, terms).astype(BF16)


def keep_kernel(plan, group, g, left, got, *rest):
    outs, terms = rest[:-1], rest[-1]
    for j, d in enumerate(group):
        value = packed_chunk(plan, chunk_index(d, False), left, g, terms) + got[j].astype(F32)
        outs[j][...] = value.astype(outs[j].dtype)


def square_kernel(scale, keep, *rest):
    value = keep[...]
    for block in rest[:-1]:
        value = value + block[...].astype(F32)
    rest[-1][...] = (value * scale).astype(BF16)


def pair_kernel(mine, got, out):
    out[...] = (mine[...].astype(F32) + got[...].astype(F32)).astype(BF16)


def final_kernel(chunk, CO, mine, got, out, total, even):
    total[...] = mine[...].astype(F32) + got[...].astype(F32)
    half, low = chunk // 2, CO - 128
    side = total[chunk:]
    even[:half, :low] = side[:, :low]
    even[half:, :low] = side[:, low:]
    a, b = (total[pl.ds(p, half, stride=2), :] for p in range(2))
    a_side, b_side = (even[pl.ds(p, half, stride=2), :][:, :low] for p in range(2))
    out[pl.ds(0, half, stride=3), :] = a
    out[pl.ds(1, half, stride=3), :] = jnp.concatenate([a_side, b[:, :low]], axis=1)
    out[pl.ds(2, half, stride=3), :] = jnp.concatenate([b[:, low:], b_side], axis=1)


def order_kernel(sizes, order, *rest):
    S, rW, n_row, _ = sizes
    bands, natural, first = rest[:n_row], rest[n_row], rest[n_row + 1]
    me = lax.axis_index("row")
    for d in range(n_row):
        source = lax.rem(me - d + n_row, n_row)
        for s in range(S):
            o = order[source * S + s]
            start = pl.multiple_of((o // 2) * rW, rW)
            natural[o % 2, pl.ds(start, rW), :] = bands[d][s]
    first[...] = natural[:, : 2 * rW, :]


def input_kernel(sizes, natural, later, time_weight, out, tail):
    rW, F, C = sizes
    tail[:, : F * rW, :] = natural[...]
    n_frame = lax.axis_size("frame")
    whole = jnp.where(lax.axis_index("frame") < n_frame - 1, 1.0, 0.0)
    tail[:, F * rW :, :] = (later[...].astype(F32) * whole).astype(BF16)
    total = jnp.zeros((F * rW, C), F32)
    for k in range(3):
        for p in range(2):
            total = total + lax.dot_general(
                tail[p, (2 - k) * rW : (2 - k + F) * rW, :],
                time_weight[k, :, p * C : (p + 1) * C],
                (((1,), (1,)), ((), ())),
                preferred_element_type=F32,
            )
    out[...] = total.astype(BF16)


def direct(n_frame, n_row, n_clip):
    n_q = n_frame * n_row // 2
    return n_frame % 2 == 0 and 1 < n_q <= 8 and n_q & (n_q - 1) == 0 and n_clip > 1 and n_clip & (n_clip - 1) == 0


def local(features, time_weight, time_bias, space_weight, pixel_grads, frame_order):
    _, F, r, W, C = features.shape
    _, S, UR, UW, CO = pixel_grads.shape
    n_row, n_frame, n_clip = (lax.axis_size(a) for a in ("row", "frame", "clip"))
    HR, rW = r * n_row, r * W
    pixels = S * HR * W
    order = frame_order.reshape(-1)
    both = ("frame", "row")

    feats = features.reshape(F, rW, C)
    forward = [(i, (i + 1) % n_frame) for i in range(n_frame)]
    prior = [lax.ppermute(feats, "frame", forward)]
    own = [feats] + [
        lax.ppermute(feats, "row", [(i, (i + d) % n_row) for i in range(n_row)])
        for d in range(1, n_row)
    ]
    for d in range(1, n_row):
        route = [(i * n_row + k, j * n_row + (k + d) % n_row) for i, j in forward for k in range(n_row)]
        prior.append(lax.ppermute(feats, both, route))
    (box,) = kernel_call(
        functools.partial(matrix_kernel, W), [struct((9 * W, 8 * W), BF16)], 0, [], flops=10**10
    )
    g, *bands = kernel_call(
        functools.partial(box_kernel, (S, HR, W, C, CO, r, n_row)),
        [struct((9, pixels, CO), BF16)] + [struct((S, rW, C), BF16)] * n_row,
        0,
        [pixel_grads.reshape(S, UR * UW, CO), space_weight.transpose(0, 1, 3, 2).reshape(9, CO, C), box],
        [
            pltpu.VMEM((S, (UR + 2) * UW, CO), BF16),
            pltpu.VMEM((S, HR * W, C), BF16),
            pltpu.VMEM((9, CO, C), BF16),
            pltpu.SemaphoreType.DMA,
            pltpu.SemaphoreType.DMA,
        ],
        far=(0, 1),
        flops=2 * pixels * 9 * C * CO,
    )

    n_total = 9 * C
    n_dev = n_frame * n_row
    n_q = n_dev // 2
    chunk = n_total // n_dev
    fast = (
        direct(n_frame, n_row, n_clip)
        and n_total % n_dev == 0
        and chunk % 16 == 0
        and CO == 192
    )
    packed = chunk * CO // 128
    sizes = (S, rW, n_row, F, C)
    bias = time_bias.reshape(-1, 128)
    (late,) = kernel_call(
        functools.partial(late_kernel, sizes),
        [struct((2, F - 2, HR * W, C), BF16)],
        0,
        [bias, time_weight] + own,
        [pltpu.VMEM((F * HR * W, C), BF16)],
        flops=2 * (F - 2) * HR * W * 6 * C * C,
    )
    inputs = [order, bias, time_weight, late, g] + own + prior
    ext = [
        pltpu.VMEM((4 * HR * W, C), BF16),
        pltpu.VMEM((2, 2, HR * W, C), BF16),
        pltpu.VMEM((pixels, C), BF16),
    ]
    flops = 2 * pixels * 9 * C * CO

    scale = 1.0 / math.sqrt(2 * F * UR * UW * n_clip * n_frame)
    if fast:
        plan = (n_dev, chunk, C, CO)
        terms = pltpu.VMEM((chunk, CO), F32)
        groups = [[n_q - 1], list(range(1, n_q - 1)), [0]]
        groups = [group for group in groups if group]
        swap = [(i, ((i // n_row) ^ 1) * n_row + i % n_row) for i in range(n_dev)]

        def square(i, d):
            f, j = i // n_row, i % n_row
            p = ((f // 2) * n_row + j) ^ d
            return ((p // n_row) * 2 + f % 2) * n_row + p % n_row

        got = []
        for k, group in enumerate(groups):
            left_out = [] if k else [struct((C, pixels), BF16)]
            *first, send = kernel_call(
                functools.partial(send_kernel, None if k else sizes, plan, group),
                left_out + [struct((len(group), packed, 128), BF16)],
                0 if k else 1,
                [g, left] if k else inputs,
                [terms] if k else ext + [terms],
                flops=flops * len(group) // n_dev,
            )
            left = left if k else first[0]
            swapped = lax.ppermute(send, both, swap)
            shares = kernel_call(
                functools.partial(keep_kernel, plan, group),
                [struct((packed, 128), BF16 if d else F32) for d in group],
                0,
                [g, left, swapped],
                [terms],
                flops=flops * len(group) // n_dev,
            )
            for d, share in zip(group, shares):
                if d:
                    route = [(i, square(i, d)) for i in range(n_dev)]
                    got.append(lax.ppermute(share, both, route))
                else:
                    mine = share
        (mine,) = kernel_call(
            functools.partial(square_kernel, scale), [struct((packed, 128), BF16)], 0, [mine] + got
        )
        masks = [(1 << k) - 1 for k in range(1, n_clip.bit_length())]
        for mask in masks:
            got = lax.ppermute(mine, "clip", [(i, i ^ mask) for i in range(n_clip)])
            if mask != masks[-1]:
                (mine,) = kernel_call(pair_kernel, [struct((packed, 128), BF16)], 0, [mine, got])
        (flat,) = kernel_call(
            functools.partial(final_kernel, chunk, CO),
            [struct((packed, 128), F32)],
            0,
            [mine, got],
            [pltpu.VMEM((packed, 128), F32), pltpu.VMEM((chunk, 128), F32)],
        )
        weight_grad = flat.reshape(-1)
    else:
        (wg,) = kernel_call(
            functools.partial(all_kernel, sizes),
            [struct((n_total, CO), F32)],
            1,
            inputs,
            ext,
            flops=flops,
        )
        shard = lax.psum_scatter(wg.reshape(-1), both, scatter_dimension=0, tiled=True)
        weight_grad = lax.psum(shard, "clip") * scale

    bands = [bands[0]] + [
        lax.ppermute(bands[d], "row", [(i, (i + d) % n_row) for i in range(n_row)])
        for d in range(1, n_row)
    ]
    natural, first = kernel_call(
        functools.partial(order_kernel, (S, rW, n_row, F)),
        [struct((2, F * rW, C), BF16), struct((2, 2 * rW, C), BF16)],
        1,
        [order] + bands,
    )
    later = lax.ppermute(first, "frame", [(j, i) for i, j in forward])
    (input_grad,) = kernel_call(
        functools.partial(input_kernel, (rW, F, C)),
        [struct((F * rW, C), BF16)],
        0,
        [natural, later, time_weight],
        [pltpu.VMEM((2, (F + 2) * rW, C), BF16)],
        flops=2 * F * rW * 6 * C * C,
    )
    return input_grad.reshape(features.shape), weight_grad


def solution(mesh):
    step = jax.shard_map(
        local,
        mesh=mesh,
        in_specs=(
            P("clip", "frame", "row", None, None),
            P(),
            P(),
            P(),
            P("clip", ("frame", "row"), None, None, None),
            P("clip", "frame", None),
        ),
        out_specs=(P("clip", "frame", "row", None, None), P(("frame", "row"))),
        check_vma=False,
    )
    if not direct(mesh.shape["frame"], mesh.shape["row"], mesh.shape["clip"]):
        return step
    return step
```

```python
import functools
import math

import jax
import jax.numpy as jnp
from jax import lax
from jax.experimental import pallas as pl
from jax.experimental.pallas import tpu as pltpu
from jax.sharding import PartitionSpec as P


F32 = jnp.float32
BF16 = jnp.bfloat16
VMEM = pl.BlockSpec(memory_space=pltpu.VMEM)
SMEM = pl.BlockSpec(memory_space=pltpu.SMEM)


def struct(shape, dtype):
    return jax.ShapeDtypeStruct(shape, dtype)


def kernel_call(body, outs, n_smem, args, scratch=(), flops=0, far=()):
    moved = sum(math.prod(a.shape) * a.dtype.itemsize for a in list(args) + list(outs))
    specs = [SMEM] * n_smem + [VMEM] * (len(args) - n_smem)
    for i in far:
        specs[i] = pl.BlockSpec(memory_space=pltpu.HBM)
    return pl.pallas_call(
        body,
        out_shape=outs,
        in_specs=specs,
        out_specs=[VMEM] * len(outs),
        scratch_shapes=list(scratch),
        compiler_params=pltpu.CompilerParams(vmem_limit_bytes=16 * 2**20),
        cost_estimate=pl.CostEstimate(flops=flops, bytes_accessed=moved, transcendentals=0),
    )(*args)


def matrix_kernel(width, out):
    column = lax.broadcasted_iota(jnp.int32, (width, 8 * width), 1)
    line, col = column // (2 * width), column % (2 * width)
    first = 2 * lax.broadcasted_iota(jnp.int32, (width, 8 * width), 0) + 1
    for a in range(3):
        rows = (line == 2 - a) | (line == 3 - a)
        for b in range(3):
            inside = rows & ((col == first - b) | (col == first + 1 - b))
            t = 3 * a + b
            out[t * width : (t + 1) * width, :] = jnp.where(inside, 1.0, 0.0).astype(BF16)


def box_kernel(sizes, grads, weight_far, box, g_out, *rest):
    S, HR, W, C, CO, r, n_row = sizes
    bands, (padded, acts, weight, grads_in, weight_in) = rest[:n_row], rest[n_row:]
    line = 2 * W
    end = line * (2 * HR + 1)
    load_grads = pltpu.make_async_copy(grads, padded.at[:, line:end, :], grads_in)
    load_weight = pltpu.make_async_copy(weight_far, weight, weight_in)
    load_grads.start()
    load_weight.start()
    for s in range(S):
        padded[s, 0:line, :] = jnp.zeros((line, CO), BF16)
        padded[s, end:, :] = jnp.zeros((line, CO), BF16)
    load_grads.wait()
    matrix = box[...]
    for s in range(S):
        for R in range(HR):
            window = padded[s, 2 * R * line : (2 * R + 4) * line, :]
            sums = jnp.dot(matrix, window, preferred_element_type=F32).astype(BF16)
            at = (s * HR + R) * W
            for t in range(9):
                g_out[t, at : at + W, :] = sums[t * W : (t + 1) * W]
    load_weight.wait()
    total = jnp.zeros((S * HR * W, C), F32)
    for t in range(9):
        total = total + jnp.dot(g_out[t], weight[t], preferred_element_type=F32)
    acts[...] = total.astype(BF16).reshape(S, HR * W, C)
    me = lax.axis_index("row")
    for d in range(n_row):
        start = pl.multiple_of(lax.rem(me + d, n_row) * (r * W), r * W)
        bands[d][...] = acts[:, pl.ds(start, r * W), :]


def extended(sizes, ext, bands):
    rW, n_row = sizes[1], sizes[2]
    me = lax.axis_index("row")
    for d in range(n_row):
        source = lax.rem(me - d + n_row, n_row)
        for f, block in enumerate(bands(d)):
            start = pl.multiple_of(f * n_row * rW + source * rW, rW)
            ext[pl.ds(start, rW), :] = block


def time_conv(sizes, frames, bias, time_weight, ext, acts):
    _, rW, n_row, _, C = sizes
    step = n_row * rW
    row = jnp.concatenate([bias[i : i + 1, :] for i in range(bias.shape[0])], axis=1)
    total = jnp.broadcast_to(row, (frames * step, 2 * C))
    for k in range(3):
        total = total + jnp.dot(
            ext[k * step : (k + frames) * step, :], time_weight[k], preferred_element_type=F32
        )
    rounded = total.astype(BF16).reshape(frames, step, 2 * C)
    acts[0] = rounded[:, :, :C]
    acts[1] = rounded[:, :, C:]


def late_kernel(sizes, bias, time_weight, *rest):
    n_row, F = sizes[2], sizes[3]
    own, (acts, ext) = rest[:n_row], rest[n_row:]
    extended(sizes, ext, lambda d: [own[d][f] for f in range(F)])
    time_conv(sizes, F - 2, bias, time_weight, ext, acts)


def transposed_acts(sizes, order, bias, time_weight, late, bands, ext, early, picked):
    S, rW, n_row, F, _ = sizes
    step = n_row * rW
    own, prior = bands[:n_row], bands[n_row:]
    whole = jnp.where(lax.axis_index("frame") > 0, 1.0, 0.0)

    def frames(d):
        before = [(prior[d][f].astype(F32) * whole).astype(BF16) for f in range(F - 2, F)]
        return before + [own[d][f] for f in range(2)]

    extended(sizes, ext, frames)
    time_conv(sizes, 2, bias, time_weight, ext, early)
    me = lax.axis_index("row")
    for s in range(S):
        o = order[me * S + s]
        f = o // 2

        @pl.when(f < 2)
        def _():
            picked[s * step : (s + 1) * step, :] = early[o % 2, f]

        @pl.when(f >= 2)
        def _():
            picked[s * step : (s + 1) * step, :] = late[o % 2, f - 2]

    return picked[...].astype(F32).T.astype(BF16)


def all_kernel(sizes, order, bias, time_weight, late, g, *rest):
    n_row, C = sizes[2], sizes[4]
    out, *scratch = rest[2 * n_row :]
    left = transposed_acts(sizes, order, bias, time_weight, late, rest[: 2 * n_row], *scratch)
    for t in range(9):
        out[t * C : (t + 1) * C, :] = jnp.dot(left, g[t], preferred_element_type=F32)


def packed_chunk(plan, index, left, g, terms):
    n_dev, chunk, C, _ = plan
    for value in range(n_dev):

        @pl.when(index == value)
        def _():
            begin, end = value * chunk, (value + 1) * chunk
            for t in range(begin // C, (end + C - 1) // C):
                lo, hi = max(begin, t * C), min(end, (t + 1) * C)
                terms[lo - begin : hi - begin, :] = jnp.dot(
                    left[lo - t * C : hi - t * C, :], g[t], preferred_element_type=F32
                )

    half = chunk // 2
    side = jnp.concatenate([terms[:half, 128:], terms[half:, 128:]], axis=1)
    return jnp.concatenate([terms[:, :128], side], axis=0)


def chunk_index(d, other):
    n_row = lax.axis_size("row")
    frame = lax.axis_index("frame")
    q = jnp.bitwise_xor((frame // 2) * n_row + lax.axis_index("row"), d)
    core = lax.rem(frame, 2)
    return ((q // n_row) * 2 + (1 - core if other else core)) * n_row + lax.rem(q, n_row)


def send_kernel(sizes, plan, group, *rest):
    if sizes:
        order, bias, time_weight, late, g, *rest = rest
        n_row = sizes[2]
        left, out, *scratch, terms = rest[2 * n_row :]
        left[...] = transposed_acts(sizes, order, bias, time_weight, late, rest[: 2 * n_row], *scratch)
    else:
        g, left, out, terms = rest
    for j, d in enumerate(group):
        out[j] = packed_chunk(plan, chunk_index(d, True), left, g, terms).astype(BF16)


def keep_kernel(plan, group, g, left, got, *rest):
    outs, terms = rest[:-1], rest[-1]
    for j, d in enumerate(group):
        value = packed_chunk(plan, chunk_index(d, False), left, g, terms) + got[j].astype(F32)
        outs[j][...] = value.astype(outs[j].dtype)


def square_kernel(scale, keep, *rest):
    value = keep[...]
    for block in rest[:-1]:
        value = value + block[...].astype(F32)
    rest[-1][...] = (value * scale).astype(BF16)


def pair_kernel(mine, got, out):
    out[...] = (mine[...].astype(F32) + got[...].astype(F32)).astype(BF16)


def final_kernel(chunk, CO, mine, got, out, total):
    total[...] = mine[...].astype(F32) + got[...].astype(F32)
    low = CO - 128
    part = chunk // 4

    def lines(start):
        return total[pl.ds(start, part, stride=2), :]

    side, side_next = lines(chunk), lines(chunk + 1)
    for h in range(2):
        a, b = lines(2 * part * h), lines(2 * part * h + 1)
        a_side, b_side = (x[:, h * low : (h + 1) * low] for x in (side, side_next))
        start = 3 * part * h
        out[pl.ds(start, part, stride=3), :] = a
        out[pl.ds(start + 1, part, stride=3), :] = jnp.concatenate([a_side, b[:, :low]], axis=1)
        out[pl.ds(start + 2, part, stride=3), :] = jnp.concatenate([b[:, low:], b_side], axis=1)


def order_kernel(sizes, order, *rest):
    S, rW, n_row, _ = sizes
    bands, natural, first = rest[:n_row], rest[n_row], rest[n_row + 1]
    me = lax.axis_index("row")
    for d in range(n_row):
        source = lax.rem(me - d + n_row, n_row)
        for s in range(S):
            o = order[source * S + s]
            start = pl.multiple_of((o // 2) * rW, rW)
            natural[o % 2, pl.ds(start, rW), :] = bands[d][s]
    first[...] = natural[:, : 2 * rW, :]


def input_kernel(sizes, natural, later, time_weight, out, tail):
    rW, F, C = sizes
    tail[:, : F * rW, :] = natural[...]
    n_frame = lax.axis_size("frame")
    whole = jnp.where(lax.axis_index("frame") < n_frame - 1, 1.0, 0.0)
    tail[:, F * rW :, :] = (later[...].astype(F32) * whole).astype(BF16)
    total = jnp.zeros((F * rW, C), F32)
    for k in range(3):
        for p in range(2):
            total = total + lax.dot_general(
                tail[p, (2 - k) * rW : (2 - k + F) * rW, :],
                time_weight[k, :, p * C : (p + 1) * C],
                (((1,), (1,)), ((), ())),
                preferred_element_type=F32,
            )
    out[...] = total.astype(BF16)


def direct(n_frame, n_row, n_clip):
    n_q = n_frame * n_row // 2
    return n_frame % 2 == 0 and 1 < n_q <= 8 and n_q & (n_q - 1) == 0 and n_clip > 1 and n_clip & (n_clip - 1) == 0


def local(features, time_weight, time_bias, space_weight, pixel_grads, frame_order):
    _, F, r, W, C = features.shape
    _, S, UR, UW, CO = pixel_grads.shape
    n_row, n_frame, n_clip = (lax.axis_size(a) for a in ("row", "frame", "clip"))
    HR, rW = r * n_row, r * W
    pixels = S * HR * W
    order = frame_order.reshape(-1)
    both = ("frame", "row")

    feats = features.reshape(F, rW, C)
    forward = [(i, (i + 1) % n_frame) for i in range(n_frame)]
    prior = [lax.ppermute(feats, "frame", forward)]
    own = [feats] + [
        lax.ppermute(feats, "row", [(i, (i + d) % n_row) for i in range(n_row)])
        for d in range(1, n_row)
    ]
    for d in range(1, n_row):
        route = [(i * n_row + k, j * n_row + (k + d) % n_row) for i, j in forward for k in range(n_row)]
        prior.append(lax.ppermute(feats, both, route))
    (box,) = kernel_call(
        functools.partial(matrix_kernel, W), [struct((9 * W, 8 * W), BF16)], 0, [], flops=10**10
    )
    g, *bands = kernel_call(
        functools.partial(box_kernel, (S, HR, W, C, CO, r, n_row)),
        [struct((9, pixels, CO), BF16)] + [struct((S, rW, C), BF16)] * n_row,
        0,
        [pixel_grads.reshape(S, UR * UW, CO), space_weight.transpose(0, 1, 3, 2).reshape(9, CO, C), box],
        [
            pltpu.VMEM((S, (UR + 2) * UW, CO), BF16),
            pltpu.VMEM((S, HR * W, C), BF16),
            pltpu.VMEM((9, CO, C), BF16),
            pltpu.SemaphoreType.DMA,
            pltpu.SemaphoreType.DMA,
        ],
        far=(0, 1),
        flops=2 * pixels * 9 * C * CO,
    )

    n_total = 9 * C
    n_dev = n_frame * n_row
    n_q = n_dev // 2
    chunk = n_total // n_dev
    fast = (
        direct(n_frame, n_row, n_clip)
        and n_total % n_dev == 0
        and chunk % 16 == 0
        and CO == 192
    )
    packed = chunk * CO // 128
    sizes = (S, rW, n_row, F, C)
    bias = time_bias.reshape(-1, 128)
    (late,) = kernel_call(
        functools.partial(late_kernel, sizes),
        [struct((2, F - 2, HR * W, C), BF16)],
        0,
        [bias, time_weight] + own,
        [pltpu.VMEM((F * HR * W, C), BF16)],
        flops=2 * (F - 2) * HR * W * 6 * C * C,
    )
    inputs = [order, bias, time_weight, late, g] + own + prior
    ext = [
        pltpu.VMEM((4 * HR * W, C), BF16),
        pltpu.VMEM((2, 2, HR * W, C), BF16),
        pltpu.VMEM((pixels, C), BF16),
    ]
    flops = 2 * pixels * 9 * C * CO

    scale = 1.0 / math.sqrt(2 * F * UR * UW * n_clip * n_frame)
    if fast:
        plan = (n_dev, chunk, C, CO)
        terms = pltpu.VMEM((chunk, CO), F32)
        groups = [[n_q - 1], list(range(1, n_q - 1)), [0]]
        groups = [group for group in groups if group]
        swap = [(i, ((i // n_row) ^ 1) * n_row + i % n_row) for i in range(n_dev)]

        def square(i, d):
            f, j = i // n_row, i % n_row
            p = ((f // 2) * n_row + j) ^ d
            return ((p // n_row) * 2 + f % 2) * n_row + p % n_row

        got = []
        for k, group in enumerate(groups):
            left_out = [] if k else [struct((C, pixels), BF16)]
            *first, send = kernel_call(
                functools.partial(send_kernel, None if k else sizes, plan, group),
                left_out + [struct((len(group), packed, 128), BF16)],
                0 if k else 1,
                [g, left] if k else inputs,
                [terms] if k else ext + [terms],
                flops=flops * len(group) // n_dev,
            )
            left = left if k else first[0]
            swapped = lax.ppermute(send, both, swap)
            shares = kernel_call(
                functools.partial(keep_kernel, plan, group),
                [struct((packed, 128), BF16 if d else F32) for d in group],
                0,
                [g, left, swapped],
                [terms],
                flops=flops * len(group) // n_dev,
            )
            for d, share in zip(group, shares):
                if d:
                    route = [(i, square(i, d)) for i in range(n_dev)]
                    got.append(lax.ppermute(share, both, route))
                else:
                    mine = share
        (mine,) = kernel_call(
            functools.partial(square_kernel, scale), [struct((packed, 128), BF16)], 0, [mine] + got
        )
        masks = [(1 << k) - 1 for k in range(1, n_clip.bit_length())]
        for mask in masks:
            got = lax.ppermute(mine, "clip", [(i, i ^ mask) for i in range(n_clip)])
            if mask != masks[-1]:
                (mine,) = kernel_call(pair_kernel, [struct((packed, 128), BF16)], 0, [mine, got])
        (flat,) = kernel_call(
            functools.partial(final_kernel, chunk, CO),
            [struct((packed, 128), F32)],
            0,
            [mine, got],
            [pltpu.VMEM((packed, 128), F32)],
        )
        weight_grad = flat.reshape(-1)
    else:
        (wg,) = kernel_call(
            functools.partial(all_kernel, sizes),
            [struct((n_total, CO), F32)],
            1,
            inputs,
            ext,
            flops=flops,
        )
        shard = lax.psum_scatter(wg.reshape(-1), both, scatter_dimension=0, tiled=True)
        weight_grad = lax.psum(shard, "clip") * scale

    bands = [bands[0]] + [
        lax.ppermute(bands[d], "row", [(i, (i + d) % n_row) for i in range(n_row)])
        for d in range(1, n_row)
    ]
    natural, first = kernel_call(
        functools.partial(order_kernel, (S, rW, n_row, F)),
        [struct((2, F * rW, C), BF16), struct((2, 2 * rW, C), BF16)],
        1,
        [order] + bands,
    )
    later = lax.ppermute(first, "frame", [(j, i) for i, j in forward])
    (input_grad,) = kernel_call(
        functools.partial(input_kernel, (rW, F, C)),
        [struct((F * rW, C), BF16)],
        0,
        [natural, later, time_weight],
        [pltpu.VMEM((2, (F + 2) * rW, C), BF16)],
        flops=2 * F * rW * 6 * C * C,
    )
    return input_grad.reshape(features.shape), weight_grad


def solution(mesh):
    step = jax.shard_map(
        local,
        mesh=mesh,
        in_specs=(
            P("clip", "frame", "row", None, None),
            P(),
            P(),
            P(),
            P("clip", ("frame", "row"), None, None, None),
            P("clip", "frame", None),
        ),
        out_specs=(P("clip", "frame", "row", None, None), P(("frame", "row"))),
        check_vma=False,
    )
    if not direct(mesh.shape["frame"], mesh.shape["row"], mesh.shape["clip"]):
        return step
    return step
```

```python
import functools
import math

import jax
import jax.numpy as jnp
from jax import lax
from jax.experimental import pallas as pl
from jax.experimental.pallas import tpu as pltpu
from jax.sharding import PartitionSpec as P


F32 = jnp.float32
BF16 = jnp.bfloat16
VMEM = pl.BlockSpec(memory_space=pltpu.VMEM)
SMEM = pl.BlockSpec(memory_space=pltpu.SMEM)


def struct(shape, dtype):
    return jax.ShapeDtypeStruct(shape, dtype)


def kernel_call(body, outs, n_smem, args, scratch=(), flops=0, far=()):
    moved = sum(math.prod(a.shape) * a.dtype.itemsize for a in list(args) + list(outs))
    specs = [SMEM] * n_smem + [VMEM] * (len(args) - n_smem)
    for i in far:
        specs[i] = pl.BlockSpec(memory_space=pltpu.HBM)
    return pl.pallas_call(
        body,
        out_shape=outs,
        in_specs=specs,
        out_specs=[VMEM] * len(outs),
        scratch_shapes=list(scratch),
        compiler_params=pltpu.CompilerParams(vmem_limit_bytes=16 * 2**20),
        cost_estimate=pl.CostEstimate(flops=flops, bytes_accessed=moved, transcendentals=0),
    )(*args)


def matrix_kernel(width, out):
    column = lax.broadcasted_iota(jnp.int32, (width, 8 * width), 1)
    line, col = column // (2 * width), column % (2 * width)
    first = 2 * lax.broadcasted_iota(jnp.int32, (width, 8 * width), 0) + 1
    for a in range(3):
        rows = (line == 2 - a) | (line == 3 - a)
        for b in range(3):
            inside = rows & ((col == first - b) | (col == first + 1 - b))
            t = 3 * a + b
            out[t * width : (t + 1) * width, :] = jnp.where(inside, 1.0, 0.0).astype(BF16)


def box_kernel(sizes, grads, weight_far, box, g_out, *rest):
    S, HR, W, C, CO, r, n_row = sizes
    bands, (padded, acts, weight, grads_in, weight_in) = rest[:n_row], rest[n_row:]
    line = 2 * W
    end = line * (2 * HR + 1)
    load_grads = pltpu.make_async_copy(grads, padded.at[:, line:end, :], grads_in)
    load_weight = pltpu.make_async_copy(weight_far, weight, weight_in)
    load_grads.start()
    load_weight.start()
    for s in range(S):
        padded[s, 0:line, :] = jnp.zeros((line, CO), BF16)
        padded[s, end:, :] = jnp.zeros((line, CO), BF16)
    load_grads.wait()
    matrix = box[...]
    for s in range(S):
        for R in range(HR):
            window = padded[s, 2 * R * line : (2 * R + 4) * line, :]
            sums = jnp.dot(matrix, window, preferred_element_type=F32).astype(BF16)
            at = (s * HR + R) * W
            for t in range(9):
                g_out[t, at : at + W, :] = sums[t * W : (t + 1) * W]
    load_weight.wait()
    total = jnp.zeros((S * HR * W, C), F32)
    for t in range(9):
        total = total + jnp.dot(g_out[t], weight[t], preferred_element_type=F32)
    acts[...] = total.astype(BF16).reshape(S, HR * W, C)
    me = lax.axis_index("row")
    for d in range(n_row):
        start = pl.multiple_of(lax.rem(me + d, n_row) * (r * W), r * W)
        bands[d][...] = acts[:, pl.ds(start, r * W), :]


def extended(sizes, ext, bands):
    rW, n_row = sizes[1], sizes[2]
    me = lax.axis_index("row")
    for d in range(n_row):
        source = lax.rem(me - d + n_row, n_row)
        for f, block in enumerate(bands(d)):
            start = pl.multiple_of(f * n_row * rW + source * rW, rW)
            ext[pl.ds(start, rW), :] = block


def time_conv(sizes, frames, bias, time_weight, ext, acts):
    _, rW, n_row, _, C = sizes
    step = n_row * rW
    row = jnp.concatenate([bias[i : i + 1, :] for i in range(bias.shape[0])], axis=1)
    total = jnp.broadcast_to(row, (frames * step, 2 * C))
    for k in range(3):
        total = total + jnp.dot(
            ext[k * step : (k + frames) * step, :], time_weight[k], preferred_element_type=F32
        )
    rounded = total.astype(BF16).reshape(frames, step, 2 * C)
    acts[0] = rounded[:, :, :C]
    acts[1] = rounded[:, :, C:]


def late_kernel(sizes, bias, time_weight, *rest):
    n_row, F = sizes[2], sizes[3]
    own, (acts, ext) = rest[:n_row], rest[n_row:]
    extended(sizes, ext, lambda d: [own[d][f] for f in range(F)])
    time_conv(sizes, F - 2, bias, time_weight, ext, acts)


def transposed_acts(sizes, order, bias, time_weight, late, bands, ext, early, picked):
    S, rW, n_row, F, _ = sizes
    step = n_row * rW
    own, prior = bands[:n_row], bands[n_row:]
    whole = jnp.where(lax.axis_index("frame") > 0, 1.0, 0.0)

    def frames(d):
        before = [(prior[d][f].astype(F32) * whole).astype(BF16) for f in range(F - 2, F)]
        return before + [own[d][f] for f in range(2)]

    extended(sizes, ext, frames)
    time_conv(sizes, 2, bias, time_weight, ext, early)
    me = lax.axis_index("row")
    for s in range(S):
        o = order[me * S + s]
        f = o // 2

        @pl.when(f < 2)
        def _():
            picked[s * step : (s + 1) * step, :] = early[o % 2, f]

        @pl.when(f >= 2)
        def _():
            picked[s * step : (s + 1) * step, :] = late[o % 2, f - 2]

    return picked[...].astype(F32).T.astype(BF16)


def all_kernel(sizes, order, bias, time_weight, late, g, *rest):
    n_row, C = sizes[2], sizes[4]
    out, *scratch = rest[2 * n_row :]
    left = transposed_acts(sizes, order, bias, time_weight, late, rest[: 2 * n_row], *scratch)
    for t in range(9):
        out[t * C : (t + 1) * C, :] = jnp.dot(left, g[t], preferred_element_type=F32)


def packed_chunk(plan, index, left, g, terms):
    n_dev, chunk, C, _ = plan
    for value in range(n_dev):

        @pl.when(index == value)
        def _():
            begin, end = value * chunk, (value + 1) * chunk
            for t in range(begin // C, (end + C - 1) // C):
                lo, hi = max(begin, t * C), min(end, (t + 1) * C)
                terms[lo - begin : hi - begin, :] = jnp.dot(
                    left[lo - t * C : hi - t * C, :], g[t], preferred_element_type=F32
                )

    half = chunk // 2
    side = jnp.concatenate([terms[:half, 128:], terms[half:, 128:]], axis=1)
    return jnp.concatenate([terms[:, :128], side], axis=0)


def step_mask(d, core, n_dev):
    if n_dev > 4 and d in (1, 2):
        return 1 + core if d == 1 else 2 - core
    return d


def chunk_index(d, other, n_dev):
    n_row = lax.axis_size("row")
    frame = lax.axis_index("frame")
    core = lax.rem(frame, 2)
    core = 1 - core if other else core
    q = (frame // 2) * n_row + lax.axis_index("row")
    q = jnp.bitwise_xor(q, step_mask(d, core, n_dev))
    return ((q // n_row) * 2 + core) * n_row + lax.rem(q, n_row)


def send_kernel(sizes, plan, group, *rest):
    if sizes:
        order, bias, time_weight, late, g, *rest = rest
        n_row = sizes[2]
        left, out, *scratch, terms = rest[2 * n_row :]
        left[...] = transposed_acts(sizes, order, bias, time_weight, late, rest[: 2 * n_row], *scratch)
    else:
        g, left, out, terms = rest
    for j, d in enumerate(group):
        out[j] = packed_chunk(plan, chunk_index(d, True, plan[0]), left, g, terms).astype(BF16)


def keep_kernel(plan, group, g, left, got, *rest):
    outs, terms = rest[:-1], rest[-1]
    for j, d in enumerate(group):
        value = packed_chunk(plan, chunk_index(d, False, plan[0]), left, g, terms) + got[j].astype(F32)
        outs[j][...] = value.astype(outs[j].dtype)


def square_kernel(scale, keep, *rest):
    value = keep[...]
    for block in rest[:-1]:
        value = value + block[...].astype(F32)
    rest[-1][...] = (value * scale).astype(BF16)


def pair_kernel(mine, got, out):
    out[...] = (mine[...].astype(F32) + got[...].astype(F32)).astype(BF16)


def final_kernel(chunk, CO, mine, got, out, total):
    total[...] = mine[...].astype(F32) + got[...].astype(F32)
    low = CO - 128
    part = chunk // 4

    def lines(start):
        return total[pl.ds(start, part, stride=2), :]

    side, side_next = lines(chunk), lines(chunk + 1)
    for h in range(2):
        a, b = lines(2 * part * h), lines(2 * part * h + 1)
        a_side, b_side = (x[:, h * low : (h + 1) * low] for x in (side, side_next))
        start = 3 * part * h
        out[pl.ds(start, part, stride=3), :] = a
        out[pl.ds(start + 1, part, stride=3), :] = jnp.concatenate([a_side, b[:, :low]], axis=1)
        out[pl.ds(start + 2, part, stride=3), :] = jnp.concatenate([b[:, low:], b_side], axis=1)


def order_kernel(sizes, order, *rest):
    S, rW, n_row, _ = sizes
    bands, natural, first = rest[:n_row], rest[n_row], rest[n_row + 1]
    me = lax.axis_index("row")
    for d in range(n_row):
        source = lax.rem(me - d + n_row, n_row)
        for s in range(S):
            o = order[source * S + s]
            start = pl.multiple_of((o // 2) * rW, rW)
            natural[o % 2, pl.ds(start, rW), :] = bands[d][s]
    first[...] = natural[:, : 2 * rW, :]


def input_kernel(sizes, natural, later, time_weight, out, tail):
    rW, F, C = sizes
    tail[:, : F * rW, :] = natural[...]
    n_frame = lax.axis_size("frame")
    whole = jnp.where(lax.axis_index("frame") < n_frame - 1, 1.0, 0.0)
    tail[:, F * rW :, :] = (later[...].astype(F32) * whole).astype(BF16)
    total = jnp.zeros((F * rW, C), F32)
    for k in range(3):
        for p in range(2):
            total = total + lax.dot_general(
                tail[p, (2 - k) * rW : (2 - k + F) * rW, :],
                time_weight[k, :, p * C : (p + 1) * C],
                (((1,), (1,)), ((), ())),
                preferred_element_type=F32,
            )
    out[...] = total.astype(BF16)


def direct(n_frame, n_row, n_clip):
    n_q = n_frame * n_row // 2
    return n_frame % 2 == 0 and 1 < n_q <= 8 and n_q & (n_q - 1) == 0 and n_clip > 1 and n_clip & (n_clip - 1) == 0


def local(features, time_weight, time_bias, space_weight, pixel_grads, frame_order):
    _, F, r, W, C = features.shape
    _, S, UR, UW, CO = pixel_grads.shape
    n_row, n_frame, n_clip = (lax.axis_size(a) for a in ("row", "frame", "clip"))
    HR, rW = r * n_row, r * W
    pixels = S * HR * W
    order = frame_order.reshape(-1)
    both = ("frame", "row")

    feats = features.reshape(F, rW, C)
    forward = [(i, (i + 1) % n_frame) for i in range(n_frame)]
    prior = [lax.ppermute(feats, "frame", forward)]
    own = [feats] + [
        lax.ppermute(feats, "row", [(i, (i + d) % n_row) for i in range(n_row)])
        for d in range(1, n_row)
    ]
    for d in range(1, n_row):
        route = [(i * n_row + k, j * n_row + (k + d) % n_row) for i, j in forward for k in range(n_row)]
        prior.append(lax.ppermute(feats, both, route))
    (box,) = kernel_call(
        functools.partial(matrix_kernel, W), [struct((9 * W, 8 * W), BF16)], 0, [], flops=10**10
    )
    g, *bands = kernel_call(
        functools.partial(box_kernel, (S, HR, W, C, CO, r, n_row)),
        [struct((9, pixels, CO), BF16)] + [struct((S, rW, C), BF16)] * n_row,
        0,
        [pixel_grads.reshape(S, UR * UW, CO), space_weight.transpose(0, 1, 3, 2).reshape(9, CO, C), box],
        [
            pltpu.VMEM((S, (UR + 2) * UW, CO), BF16),
            pltpu.VMEM((S, HR * W, C), BF16),
            pltpu.VMEM((9, CO, C), BF16),
            pltpu.SemaphoreType.DMA,
            pltpu.SemaphoreType.DMA,
        ],
        far=(0, 1),
        flops=2 * pixels * 9 * C * CO,
    )

    n_total = 9 * C
    n_dev = n_frame * n_row
    n_q = n_dev // 2
    chunk = n_total // n_dev
    fast = (
        direct(n_frame, n_row, n_clip)
        and n_total % n_dev == 0
        and chunk % 16 == 0
        and CO == 192
    )
    packed = chunk * CO // 128
    sizes = (S, rW, n_row, F, C)
    bias = time_bias.reshape(-1, 128)
    (late,) = kernel_call(
        functools.partial(late_kernel, sizes),
        [struct((2, F - 2, HR * W, C), BF16)],
        0,
        [bias, time_weight] + own,
        [pltpu.VMEM((F * HR * W, C), BF16)],
        flops=2 * (F - 2) * HR * W * 6 * C * C,
    )
    inputs = [order, bias, time_weight, late, g] + own + prior
    ext = [
        pltpu.VMEM((4 * HR * W, C), BF16),
        pltpu.VMEM((2, 2, HR * W, C), BF16),
        pltpu.VMEM((pixels, C), BF16),
    ]
    flops = 2 * pixels * 9 * C * CO

    scale = 1.0 / math.sqrt(2 * F * UR * UW * n_clip * n_frame)
    if fast:
        plan = (n_dev, chunk, C, CO)
        terms = pltpu.VMEM((chunk, CO), F32)
        groups = [[n_q - 1], list(range(1, n_q - 1)), [0]]
        groups = [group for group in groups if group]
        swap = [(i, ((i // n_row) ^ 1) * n_row + i % n_row) for i in range(n_dev)]

        def square(i, d):
            f, j = i // n_row, i % n_row
            p = ((f // 2) * n_row + j) ^ step_mask(d, f % 2, n_dev)
            return ((p // n_row) * 2 + f % 2) * n_row + p % n_row

        got = []
        for k, group in enumerate(groups):
            left_out = [] if k else [struct((C, pixels), BF16)]
            *first, send = kernel_call(
                functools.partial(send_kernel, None if k else sizes, plan, group),
                left_out + [struct((len(group), packed, 128), BF16)],
                0 if k else 1,
                [g, left] if k else inputs,
                [terms] if k else ext + [terms],
                flops=flops * len(group) // n_dev,
            )
            left = left if k else first[0]
            swapped = lax.ppermute(send, both, swap)
            shares = kernel_call(
                functools.partial(keep_kernel, plan, group),
                [struct((packed, 128), BF16 if d else F32) for d in group],
                0,
                [g, left, swapped],
                [terms],
                flops=flops * len(group) // n_dev,
            )
            for d, share in zip(group, shares):
                if d:
                    route = [(i, square(i, d)) for i in range(n_dev)]
                    got.append(lax.ppermute(share, both, route))
                else:
                    mine = share
        (mine,) = kernel_call(
            functools.partial(square_kernel, scale), [struct((packed, 128), BF16)], 0, [mine] + got
        )
        masks = [(1 << k) - 1 for k in range(1, n_clip.bit_length())]
        for mask in masks:
            got = lax.ppermute(mine, "clip", [(i, i ^ mask) for i in range(n_clip)])
            if mask != masks[-1]:
                (mine,) = kernel_call(pair_kernel, [struct((packed, 128), BF16)], 0, [mine, got])
        (flat,) = kernel_call(
            functools.partial(final_kernel, chunk, CO),
            [struct((packed, 128), F32)],
            0,
            [mine, got],
            [pltpu.VMEM((packed, 128), F32)],
        )
        weight_grad = flat.reshape(-1)
    else:
        (wg,) = kernel_call(
            functools.partial(all_kernel, sizes),
            [struct((n_total, CO), F32)],
            1,
            inputs,
            ext,
            flops=flops,
        )
        shard = lax.psum_scatter(wg.reshape(-1), both, scatter_dimension=0, tiled=True)
        weight_grad = lax.psum(shard, "clip") * scale

    bands = [bands[0]] + [
        lax.ppermute(bands[d], "row", [(i, (i + d) % n_row) for i in range(n_row)])
        for d in range(1, n_row)
    ]
    natural, first = kernel_call(
        functools.partial(order_kernel, (S, rW, n_row, F)),
        [struct((2, F * rW, C), BF16), struct((2, 2 * rW, C), BF16)],
        1,
        [order] + bands,
    )
    later = lax.ppermute(first, "frame", [(j, i) for i, j in forward])
    (input_grad,) = kernel_call(
        functools.partial(input_kernel, (rW, F, C)),
        [struct((F * rW, C), BF16)],
        0,
        [natural, later, time_weight],
        [pltpu.VMEM((2, (F + 2) * rW, C), BF16)],
        flops=2 * F * rW * 6 * C * C,
    )
    return input_grad.reshape(features.shape), weight_grad


def solution(mesh):
    step = jax.shard_map(
        local,
        mesh=mesh,
        in_specs=(
            P("clip", "frame", "row", None, None),
            P(),
            P(),
            P(),
            P("clip", ("frame", "row"), None, None, None),
            P("clip", "frame", None),
        ),
        out_specs=(P("clip", "frame", "row", None, None), P(("frame", "row"))),
        check_vma=False,
    )
    if not direct(mesh.shape["frame"], mesh.shape["row"], mesh.shape["clip"]):
        return step
    return step
```
